32 devices in a mesh: gx: 4 (over y, x), gy: 4 (over z), gz: 2 (over core).
Axes of the slice: x: 2, y: 2, z: 4, core: 2. Of those that a mesh axis runs over, the one named last changes fastest.
Arguments:
- features: bfloat16 [4, 4, 4, 128, 128], P('gx', 'gy', 'gz'), may hold values from -6 to 6
- positions: int32 [3, 4, 4, 4, 128], P(None, 'gx', 'gy', 'gz'), may hold values from 0 to 63
- wavevectors: int32 [3, 1024], replicated, may hold values from -6 to 6
- radial_mix: bfloat16 [768, 128], replicated, may hold values from -0.0546875 to 0.0546875
- charge_weight: bfloat16 [128, 128], replicated, may hold values from -0.5 to 0.5
- filters: float32 [1024, 128], replicated, may hold values from 0.01 to 0.1
- mix_weight: float32 [128, 128], replicated, may hold values from -0.5 to 0.5
- norm_gain: float32 [128], replicated, may hold values from 0.1 to 1.9
- up_weight: bfloat16 [128, 256], replicated, may hold values from -0.5 to 0.5
- down_weight: bfloat16 [256, 128], replicated, may hold values from -0.375 to 0.375
Outputs:
- updated: bfloat16 [4, 4, 4, 128, 128], P('gx', 'gy', 'gz')
The draws below stay inside these ranges and needn't reach their ends.
All inputs are finite; a program needn't handle non-finite values.
Results may differ from the reference program's by a relative error of at most 0.006.
Values may be sent and summed in bfloat16 or wider, within the bound.
No kernel may reach another device: no remote copies, remote signals or barrier semaphores. Data moves between devices by JAX's collectives and lax.ppermute only.
A program may use at most 64 MiB of HBM per device.

```python
import math
import jax
import jax.numpy as jnp
from jax import lax

D = 128
HID = 256
NRBF = 6
TILE = 128
K = 1024
GRID = 64
NTX = 4
NTY = 4
NTZ = 4


def touch_ends(values, stream_key, smallest, largest):
    spot = [jax.random.randint(jax.random.fold_in(stream_key, axis), (), 0, length) for axis, length in enumerate(values.shape)]
    longest = values.shape.index(max(values.shape))
    beside = spot[:longest] + [(spot[longest] + 1) % values.shape[longest]] + spot[longest + 1:]
    return values.at[tuple(spot)].set(smallest).at[tuple(beside)].set(largest)


def shard_levels(rng, dims, pieces, low, largest):
    level, own = 1.0, jax.random.fold_in(rng, 6)
    for axis_at, shards_of in pieces:
        steps = jnp.exp(jax.random.uniform(jax.random.fold_in(own, axis_at), (shards_of,), jnp.float32, low / len(pieces), largest / len(pieces)))
        level = level * jnp.repeat(steps, dims[axis_at] // shards_of).reshape([-1 if axis == axis_at else 1 for axis in range(len(dims))])
    return level


def scatter_about(own_key, shape, width, reach, pieces=(), kind=jnp.bfloat16):
    drawn = width * jax.random.normal(own_key, shape, jnp.float32)
    if pieces:
        drawn = drawn * shard_levels(own_key, shape, pieces, -0.22, 0.18)
    return jnp.clip(drawn, -reach, reach).astype(kind)


def setup_inputs(seed: int = 0) -> dict:
    seeds = jax.random.split(jax.random.key(seed), 11)
    return {
        "features": scatter_about(seeds[0], (NTX, NTY, NTZ, TILE, D), 1.0, 6.0, ((0, 4), (1, 4), (2, 2))),
        "positions": touch_ends(jax.random.randint(seeds[1], (3, NTX, NTY, NTZ, TILE), 0, GRID), jax.random.fold_in(seeds[1], 1), 0, GRID - 1).astype(jnp.int32),
        "wavevectors": touch_ends(jax.random.randint(seeds[2], (3, K), -6, 7), jax.random.fold_in(seeds[2], 1), -6, 6).astype(jnp.int32),
        "radial_mix": scatter_about(seeds[3], (NRBF * D, D), (16 * NRBF * D) ** -0.5, 0.0546875),
        "charge_weight": scatter_about(seeds[4], (D, D), D ** -0.5, 0.5),
        "filters": jnp.clip(jnp.exp(jax.random.uniform(seeds[5], (K, D), jnp.float32, math.log(0.01), math.log(0.1))), 0.01, 0.1),
        "mix_weight": scatter_about(seeds[6], (D, D), D ** -0.5, 0.5, (), jnp.float32),
        "norm_gain": jnp.clip(1.0 + 0.18 * jax.random.normal(seeds[7], (D,), jnp.float32), 0.1, 1.9),
        "up_weight": scatter_about(seeds[8], (D, HID), D ** -0.5, 0.5),
        "down_weight": scatter_about(seeds[9], (HID, D), HID ** -0.5, 0.375),
    }


SHARP = 18.0
TWO_PI = 2.0 * math.pi
EPS = 1e-06
CONTRACT_FIRST = (((0,), (0,)), ((), ()))

def radial_basis(center, nearby_pos):
    tile_size = center.shape[1]
    offsets = jnp.stack([lax.broadcasted_iota(jnp.int32, (3, 3, 3, 1), component) for component in range(3)]) - 1
    coords = (nearby_pos + offsets * GRID).reshape(3, 27 * tile_size)
    displace = coords[:, None, :] - center[:, :, None]
    square = lax.optimization_barrier(jnp.sum(displace * displace, axis=0))
    scaled_dist = jnp.sqrt(square.astype(jnp.float32)) / GRID
    inside = (square > 0) & (square < GRID * GRID)
    envelope = jnp.where(inside, (1.0 - scaled_dist * scaled_dist) ** 2, 0.0)
    centres = (jnp.arange(NRBF, dtype=jnp.float32) + 0.5) / NRBF
    radial = jnp.exp(-SHARP * (scaled_dist[:, None, :] - centres[None, :, None]) ** 2) * envelope[:, None, :]
    return radial.astype(jnp.bfloat16)

def tile_message(center, nearby_pos, neighbour, radial_mix):
    tile_size = center.shape[1]
    radial = radial_basis(center, nearby_pos)
    pooled = jnp.einsum('irj,jd->ird', radial.astype(jnp.float32), neighbour.astype(jnp.float32))
    pooled = pooled.astype(jnp.bfloat16).reshape(tile_size, -1)
    return jnp.dot(pooled, radial_mix, preferred_element_type=jnp.float32)

def phase_tables(wavevectors, coords, lengths):
    fraction = jnp.zeros((wavevectors.shape[1], coords.shape[1]), jnp.float32)
    for component in range(3):
        product = jnp.mod(wavevectors[component][:, None] * coords[component][None, :], lengths[component])
        fraction = fraction + product.astype(jnp.float32) / lengths[component]
    phase_angle = TWO_PI * fraction
    return (jnp.cos(phase_angle).astype(jnp.bfloat16), jnp.sin(phase_angle).astype(jnp.bfloat16))

def reference(features, positions, wavevectors, radial_mix, charge_weight, filters, mix_weight, norm_gain, up_weight, down_weight):
    count_x, count_y, count_z, tile_size, feat_width = features.shape
    pad_feat = jnp.pad(features, ((1, 1), (1, 1), (1, 1), (0, 0), (0, 0)), mode='wrap')
    pad_pos = jnp.pad(positions, ((0, 0), (1, 1), (1, 1), (1, 1), (0, 0)), mode='wrap')
    anchor = jnp.zeros((), jnp.int32)

    def one_tile(flat_index):
        tile_x = (flat_index // (count_y * count_z)).astype(jnp.int32)
        tile_y = (flat_index // count_z % count_y).astype(jnp.int32)
        tile_z = (flat_index % count_z).astype(jnp.int32)
        neighbour = lax.dynamic_slice(pad_feat, (tile_x, tile_y, tile_z, anchor, anchor), (3, 3, 3, tile_size, feat_width))
        nearby_pos = lax.dynamic_slice(pad_pos, (anchor, tile_x, tile_y, tile_z, anchor), (3, 3, 3, 3, tile_size))
        center = lax.dynamic_slice(positions, (anchor, tile_x, tile_y, tile_z, anchor), (3, 1, 1, 1, tile_size)).reshape(3, tile_size)
        return tile_message(center, nearby_pos, neighbour.reshape(27 * tile_size, feat_width), radial_mix)
    message = lax.map(one_tile, jnp.arange(count_x * count_y * count_z, dtype=jnp.int32))
    message = message.reshape(count_x, count_y, count_z, tile_size, feat_width)
    lengths = (count_x * GRID, count_y * GRID, count_z * GRID)
    charges = jnp.dot(features.reshape(-1, feat_width), charge_weight, preferred_element_type=jnp.float32)
    charges = charges.astype(jnp.bfloat16).reshape(count_x * count_y, count_z * tile_size, feat_width)

    def row_coords(row_index):
        tile_x = (row_index // count_y).astype(jnp.int32)
        tile_y = (row_index % count_y).astype(jnp.int32)
        local_pos = lax.dynamic_slice(positions, (anchor, tile_x, tile_y, anchor, anchor), (3, 1, 1, count_z, tile_size)).reshape(3, count_z, tile_size)
        zeros_int = jnp.zeros((count_z, tile_size), jnp.int32)
        tile_coord = jnp.stack([tile_x + zeros_int, tile_y + zeros_int, lax.broadcasted_iota(jnp.int32, (count_z, tile_size), 0)])
        return (tile_coord * GRID + local_pos).reshape(3, count_z * tile_size)

    def add_row(totals, row_index):
        cos_table, sin_table = phase_tables(wavevectors, row_coords(row_index), lengths)
        row_charges = charges[row_index]
        return ((totals[0] + jnp.dot(cos_table, row_charges, preferred_element_type=jnp.float32), totals[1] + jnp.dot(sin_table, row_charges, preferred_element_type=jnp.float32)), None)
    start_sums = (jnp.zeros((wavevectors.shape[1], feat_width), jnp.float32), jnp.zeros((wavevectors.shape[1], feat_width), jnp.float32))
    sums, unused = lax.scan(add_row, start_sums, jnp.arange(count_x * count_y, dtype=jnp.int32))
    scale = 1.0 / math.sqrt(count_x * count_y * count_z * tile_size)
    filtered_cos = jnp.dot(filters * (sums[0] * scale), mix_weight, precision=lax.Precision.HIGHEST).astype(jnp.bfloat16)
    filtered_sin = jnp.dot(filters * (sums[1] * scale), mix_weight, precision=lax.Precision.HIGHEST).astype(jnp.bfloat16)

    def row_long(row_index):
        cos_table, sin_table = phase_tables(wavevectors, row_coords(row_index), lengths)
        result = lax.dot_general(cos_table.astype(jnp.float32), filtered_cos.astype(jnp.float32), CONTRACT_FIRST)
        return result + lax.dot_general(sin_table.astype(jnp.float32), filtered_sin.astype(jnp.float32), CONTRACT_FIRST)
    longrange = lax.map(row_long, jnp.arange(count_x * count_y, dtype=jnp.int32))
    longrange = longrange.reshape(count_x, count_y, count_z, tile_size, feat_width)
    summed = features.astype(jnp.float32) + message + longrange
    flat_sum = summed.reshape(-1, feat_width)
    normed = flat_sum * lax.rsqrt(lax.optimization_barrier(jnp.mean(flat_sum * flat_sum, axis=-1, keepdims=True)) + EPS) * norm_gain
    hidden = jax.nn.silu(jnp.dot(normed.astype(jnp.bfloat16), up_weight, preferred_element_type=jnp.float32)).astype(jnp.bfloat16)
    updated = flat_sum + jnp.dot(hidden, down_weight, preferred_element_type=jnp.float32)
    return updated.reshape(features.shape).astype(jnp.bfloat16)
```

```python
import functools
import math

import jax
import jax.numpy as jnp
import numpy as np
from jax import lax
from jax.experimental import pallas as pl
from jax.experimental.pallas import tpu as pltpu
from jax.sharding import PartitionSpec as P

NRBF = 6
GRID = 64


SHARP = 18.0
TWO_PI = 2.0 * math.pi
EPS = 1e-06
CONTRACT_FIRST = (((0,), (0,)), ((), ()))


def extended(array, sides, width):
    for axis, dim in sides:
        size, length = (lax.axis_size(axis), array.shape[dim])
        up = [(i, (i + 1) % size) for i in range(size)]
        down = [(j, i) for i, j in up]
        last = lax.slice_in_dim(array, length - width, length, axis=dim)
        first = lax.slice_in_dim(array, 0, width, axis=dim)
        before = lax.ppermute(last, axis, up)
        after = lax.ppermute(first, axis, down)
        array = jnp.concatenate([before, array, after], axis=dim)
    return array


def radial_basis(center, nearby_pos):
    tile_size = center.shape[1]
    offsets = (
        jnp.stack(
            [lax.broadcasted_iota(jnp.int32, (3, 3, 3, 1), component) for component in range(3)]
        )
        - 1
    )
    coords = (nearby_pos + offsets * GRID).reshape(3, 27 * tile_size)
    displace = coords[:, None, :] - center[:, :, None]
    square = jnp.sum(displace * displace, axis=0)
    scaled_dist = jnp.sqrt(square.astype(jnp.float32)) / GRID
    inside = (square > 0) & (square < GRID * GRID)
    envelope = jnp.where(inside, (1.0 - scaled_dist * scaled_dist) ** 2, 0.0)
    centres = (jnp.arange(NRBF, dtype=jnp.float32) + 0.5) / NRBF
    radial = (
        jnp.exp(-SHARP * (scaled_dist[:, None, :] - centres[None, :, None]) ** 2)
        * envelope[:, None, :]
    )
    return radial.astype(jnp.bfloat16)


def phase_tables(wavevectors, coords, lengths):
    fraction = jnp.zeros((wavevectors.shape[1], coords.shape[1]), jnp.float32)
    for component in range(3):
        product = jnp.mod(
            wavevectors[component][:, None] * coords[component][None, :], lengths[component]
        )
        fraction = fraction + product.astype(jnp.float32) / lengths[component]
    phase_angle = TWO_PI * fraction
    return (jnp.cos(phase_angle).astype(jnp.bfloat16), jnp.sin(phase_angle).astype(jnp.bfloat16))


def filter_mix(filters, factor, mix_weight):
    return jnp.dot(filters * factor, mix_weight, precision=lax.Precision.HIGHEST).astype(
        jnp.bfloat16
    )


def on_device(
    features,
    positions,
    wavevectors,
    radial_mix,
    charge_weight,
    filters,
    mix_weight,
    norm_gain,
    up_weight,
    down_weight,
):
    count_x, count_y, count_z, tile_size, feat_width = features.shape
    beside_all = extended(features, (("gx", 0), ("gy", 1), ("gz", 2)), 1)
    around_pos = extended(positions, (("gx", 1), ("gy", 2), ("gz", 3)), 1)
    anchor = jnp.zeros((), jnp.int32)

    def one_tile(flat_index):
        tile_x = flat_index // (count_y * count_z)
        tile_y = flat_index // count_z % count_y
        tile_z = flat_index % count_z
        neighbour = lax.dynamic_slice(
            beside_all, (tile_x, tile_y, tile_z, anchor, anchor), (3, 3, 3, tile_size, feat_width)
        )
        nearby_pos = lax.dynamic_slice(
            around_pos, (anchor, tile_x, tile_y, tile_z, anchor), (3, 3, 3, 3, tile_size)
        )
        center = lax.dynamic_slice(
            positions, (anchor, tile_x, tile_y, tile_z, anchor), (3, 1, 1, 1, tile_size)
        ).reshape(3, tile_size)
        radial = radial_basis(center, nearby_pos)
        pooled = jnp.einsum(
            "irj,jd->ird",
            radial,
            neighbour.reshape(27 * tile_size, feat_width),
            preferred_element_type=jnp.float32,
        )
        pooled = pooled.astype(jnp.bfloat16).reshape(tile_size, -1)
        return jnp.dot(pooled, radial_mix, preferred_element_type=jnp.float32)

    message = lax.map(one_tile, jnp.arange(count_x * count_y * count_z, dtype=jnp.int32))
    message = message.reshape(count_x * count_y * count_z * tile_size, feat_width)
    atom_count = count_x * count_y * count_z * tile_size
    counts = (count_x, count_y, count_z)
    axis_sizes = (lax.axis_size("gx"), lax.axis_size("gy"), lax.axis_size("gz"))
    axis_index = (lax.axis_index("gx"), lax.axis_index("gy"), lax.axis_index("gz"))
    lengths = tuple((counts[component] * axis_sizes[component] * GRID for component in range(3)))
    coords = jnp.stack(
        [
            (
                axis_index[component] * counts[component]
                + lax.broadcasted_iota(jnp.int32, (count_x, count_y, count_z, tile_size), component)
            )
            * GRID
            + positions[component]
            for component in range(3)
        ]
    ).reshape(3, atom_count)
    cos_table, sin_table = phase_tables(wavevectors, coords, lengths)
    charges = jnp.dot(
        features.reshape(atom_count, feat_width), charge_weight, preferred_element_type=jnp.float32
    ).astype(jnp.bfloat16)
    partial_cos = jnp.dot(cos_table, charges, preferred_element_type=jnp.float32)
    partial_sin = jnp.dot(sin_table, charges, preferred_element_type=jnp.float32)
    scale = 1.0 / math.sqrt(atom_count * axis_sizes[0] * axis_sizes[1] * axis_sizes[2])
    summed_cos, summed_sin = lax.psum((partial_cos, partial_sin), ("gx", "gy", "gz"))
    filtered_cos = filter_mix(filters, summed_cos * scale, mix_weight)
    filtered_sin = filter_mix(filters, summed_sin * scale, mix_weight)
    longrange = lax.dot_general(
        cos_table, filtered_cos, CONTRACT_FIRST, preferred_element_type=jnp.float32
    )
    longrange = longrange + lax.dot_general(
        sin_table, filtered_sin, CONTRACT_FIRST, preferred_element_type=jnp.float32
    )
    flat_sum = features.reshape(atom_count, feat_width).astype(jnp.float32) + message + longrange
    normed = (
        flat_sum
        * lax.rsqrt(jnp.mean(flat_sum * flat_sum, axis=-1, keepdims=True) + EPS)
        * norm_gain
    )
    hidden = jax.nn.silu(
        jnp.dot(normed.astype(jnp.bfloat16), up_weight, preferred_element_type=jnp.float32)
    ).astype(jnp.bfloat16)
    updated = flat_sum + jnp.dot(hidden, down_weight, preferred_element_type=jnp.float32)
    return updated.reshape(features.shape).astype(jnp.bfloat16)


LOG2E = 1.4426950408889634
POS_ROWS = 16
ROUND = 12582912.0


def shift(array, axis, step):
    size = lax.axis_size(axis)
    return lax.ppermute(array, axis, [(i, (i + step) % size) for i in range(size)])


def sin_coefficients():
    nodes = np.cos((np.arange(400) + 0.5) / 400 * np.pi) * 0.25
    powers = np.stack([nodes ** (2 * n + 1) for n in range(6)], axis=1)
    scale = np.abs(powers).max(axis=0)
    fit = np.linalg.lstsq(powers / scale, np.sin(2 * np.pi * nodes), rcond=None)[0] / scale
    return [float(value) for value in fit]


SIN_FIT = sin_coefficients()


def sin_turns(u):
    square = u * u
    value = square * SIN_FIT[-1] + SIN_FIT[-2]
    for coefficient in SIN_FIT[-3::-1]:
        value = value * square + coefficient
    return value * u


def from_nearest(turns):
    return turns - ((turns + ROUND) - ROUND)


def table_kernel(n_blocks, z_tiles, place_ref, waves_ref, charge_ref, *refs):
    z_size = len(refs) - 1 - n_blocks
    columns, table_ref, parts = refs[:z_size], refs[z_size], refs[z_size + 1 :]
    tile = columns[0].shape[2]
    block = waves_ref.shape[1] // n_blocks
    row = lax.broadcasted_iota(jnp.int32, (POS_ROWS, tile), 0)
    coords, charges = [], []
    for step in range(z_size):
        for t in range(z_tiles):
            pos = columns[step][t, tile : tile + POS_ROWS, :].astype(jnp.float32)
            z = lax.rem(place_ref[2] + step, z_size) * z_tiles + t
            pos = jnp.where(row == 3, place_ref[0].astype(jnp.float32), pos)
            pos = jnp.where(row == 4, place_ref[1].astype(jnp.float32), pos)
            pos = jnp.where(row == 5, z.astype(jnp.float32), pos)
            coords.append(pos.astype(jnp.bfloat16))
            charges.append(
                jnp.dot(
                    columns[step][t, :tile, :], charge_ref[...], preferred_element_type=jnp.float32
                ).astype(jnp.bfloat16)
            )
    coords = jnp.concatenate(coords, axis=1)
    charges = jnp.concatenate(charges, axis=0)
    for n in range(n_blocks):
        turns = lax.dot_general(
            waves_ref[:, n * block : (n + 1) * block],
            coords,
            CONTRACT_FIRST,
            preferred_element_type=jnp.float32,
        )
        cos_part = sin_turns(0.25 - jnp.abs(from_nearest(turns)))
        sin_part = sin_turns(0.25 - jnp.abs(from_nearest(turns - 0.25)))
        base = 2 * n * block
        table_ref[base : base + block, :] = cos_part.astype(jnp.bfloat16)
        table_ref[base + block : base + 2 * block, :] = sin_part.astype(jnp.bfloat16)
        parts[n][...] = jnp.dot(
            table_ref[base : base + 2 * block, :], charges, preferred_element_type=jnp.float32
        ).astype(jnp.bfloat16)


def add_kernel(*refs):
    total = refs[0][...].astype(jnp.float32)
    for ref in refs[1:-1]:
        total = total + ref[...].astype(jnp.float32)
    refs[-1][...] = total.astype(refs[-1].dtype)


def mix_kernel(scale, place_ref, filters_ref, mix_ref, *refs):
    total = refs[0][...].astype(jnp.float32)
    for ref in refs[1:-1]:
        total = total + ref[...].astype(jnp.float32)
    both = jnp.concatenate([filters_ref[...], filters_ref[...]], axis=0)
    refs[-1][...] = jnp.dot(
        both * (total * scale),
        mix_ref[...],
        precision=lax.Precision.HIGHEST,
        preferred_element_type=jnp.float32,
    ).astype(jnp.bfloat16)


def rows_of(row, values):
    out = jnp.zeros(row.shape, jnp.float32)
    for n, value in enumerate(values):
        out = jnp.where(row == n, value, out)
    return out.astype(jnp.bfloat16)


def split_norm(x, y, z):
    norm = x * x + y * y + z * z
    high = jnp.floor(norm * 16.0) * 0.0625
    return high, norm - high


def radial_kernel(offsets, z_tiles, has_extra, *refs):
    own_ref, before_ref, after_ref = refs[:3]
    groups = refs[3 : 3 + len(offsets)]
    mix_ref = refs[3 + len(offsets)]
    extra_ref = refs[4 + len(offsets)] if has_extra else None
    out_ref, radial_ref, feature_ref = refs[-3:]
    tile = own_ref.shape[2]
    row = lax.broadcasted_iota(jnp.int32, (POS_ROWS, tile), 0)
    columns = [(g, c, dx, dy) for g, per in enumerate(offsets) for c, (dx, dy) in enumerate(per)]

    def unit(ref_rows):
        pos = ref_rows.astype(jnp.float32) * (1.0 / GRID)
        return pos[0:1, :], pos[1:2, :], pos[2:3, :]

    sources = {}
    for slot, (g, c, dx, dy) in enumerate(columns):
        for sz in range(z_tiles):
            x, y, z = unit(groups[g][c, sz, tile : tile + POS_ROWS, :])
            high, low = split_norm(x, y, z)
            one = jnp.ones_like(x)
            sources[slot, sz] = rows_of(row, [x, y, z, one, one, high, low])
            feature_ref[sz, slot * tile : (slot + 1) * tile, :] = groups[g][c, sz, :tile, :]
    targets = [(-1, before_ref, z_tiles - 1)]
    targets += [(t, own_ref, t) for t in range(z_tiles)]
    targets += [(z_tiles, after_ref, 0)]
    for index, (tz, ref, at) in enumerate(targets):
        x0, y0, z0 = unit(ref[at, tile : tile + POS_ROWS, :])
        near = [sz for sz in range(z_tiles) if abs(sz - tz) <= 1]
        pooled = [None] * NRBF
        for place, sz in enumerate(near):
            buffer = radial_ref.at[(index + place) % 2]
            for slot, (g, c, dx, dy) in enumerate(columns):
                x, y, z = x0 - dx, y0 - dy, z0 - (sz - tz)
                high, low = split_norm(x, y, z)
                one = jnp.ones_like(x)
                target = rows_of(row, [-2 * x, -2 * y, -2 * z, high, low, one, one])
                square = lax.dot_general(
                    target, sources[slot, sz], CONTRACT_FIRST, preferred_element_type=jnp.float32
                )
                square = jnp.where(square == 0.0, 1.0, jnp.minimum(square, 1.0))
                dist = square * lax.rsqrt(square)
                lack = 1.0 - square
                value = jnp.exp2(dist * (3.0 * LOG2E - (SHARP * LOG2E) * dist)) * (lack * lack)
                growth = jnp.exp2(dist * (6.0 * LOG2E))
                for r in range(NRBF):
                    buffer[r * tile : (r + 1) * tile, slot * tile : (slot + 1) * tile] = (
                        value.astype(jnp.bfloat16)
                    )
                    if r + 1 < NRBF:
                        value = value * growth
            part = jnp.dot(buffer[...], feature_ref[sz], preferred_element_type=jnp.float32)
            for r in range(NRBF):
                piece = part[r * tile : (r + 1) * tile, :]
                pooled[r] = piece if pooled[r] is None else pooled[r] + piece
        message = extra_ref[index] if has_extra else None
        for r in range(NRBF):
            level = math.exp(-SHARP * ((r + 0.5) / NRBF) ** 2)
            part = jnp.dot(
                (pooled[r] * level).astype(jnp.bfloat16),
                mix_ref[r * tile : (r + 1) * tile, :],
                preferred_element_type=jnp.float32,
            )
            message = part if message is None else message + part
        out_ref[index] = message


def long_kernel(z_tiles, n_blocks, table_ref, message_ref, *refs):
    blocks, outs = refs[:n_blocks], refs[n_blocks:]
    z_size, tile = len(outs), message_ref.shape[1]
    filtered = jnp.concatenate([ref[...] for ref in blocks], axis=0)
    flipped = lax.dot_general(
        filtered, table_ref[...], CONTRACT_FIRST, preferred_element_type=jnp.float32
    )
    for step in range(z_size):
        for t in range(z_tiles):
            at = (step * z_tiles + t) * tile
            value = flipped[:, at : at + tile].T
            if step == 0:
                value = value + message_ref[1 + t]
            if step == (z_size - 1) % z_size and t == z_tiles - 1:
                value = value + message_ref[0]
            if step == 1 % z_size and t == 0:
                value = value + message_ref[z_tiles + 1]
            outs[step][t * tile : (t + 1) * tile, :] = value


def node_kernel(features_ref, gain_ref, up_ref, down_ref, *refs):
    total = features_ref[...].astype(jnp.float32)
    for ref in refs[:-1]:
        total = total + ref[...]
    normed = (
        total
        * lax.rsqrt(jnp.mean(total * total, axis=-1, keepdims=True) + EPS)
        * gain_ref[...]
    )
    inner = jnp.dot(normed.astype(jnp.bfloat16), up_ref[...], preferred_element_type=jnp.float32)
    hidden = (inner / (1.0 + jnp.exp(-inner))).astype(jnp.bfloat16)
    updated = total + jnp.dot(hidden, down_ref[...], preferred_element_type=jnp.float32)
    refs[-1][...] = updated.astype(jnp.bfloat16)


def call(kernel, out_shape, *args, scalars=0, scratch=(), blocks=None, name=None):
    def whole(a):
        return pl.BlockSpec(a.shape, lambda i, *s: (0,) * len(a.shape))

    specs = [whole(a) for a in args[scalars:]]
    for at, spec in (blocks or {}).items():
        specs[at] = spec
    single = not isinstance(out_shape, (list, tuple))
    outs = whole(out_shape) if single else [whole(o) for o in out_shape]
    return pl.pallas_call(
        kernel,
        out_shape=out_shape,
        grid_spec=pltpu.PrefetchScalarGridSpec(
            num_scalar_prefetch=scalars,
            grid=(1,),
            in_specs=specs,
            out_specs=outs,
            scratch_shapes=list(scratch),
        ),
        name=name,
    )(*args)


def fast_device(
    features,
    positions,
    wavevectors,
    radial_mix,
    charge_weight,
    filters,
    mix_weight,
    norm_gain,
    up_weight,
    down_weight,
):
    z_tiles, tile, width = features.shape[2:]
    sizes = tuple(lax.axis_size(axis) for axis in ("gx", "gy", "gz"))
    place = jnp.stack([lax.axis_index(axis) for axis in ("gx", "gy", "gz")]).astype(jnp.int32)
    counts = (sizes[0], sizes[1], sizes[2] * z_tiles)
    n_blocks, waves = sizes[0], wavevectors.shape[1] // sizes[2]
    block = waves // n_blocks
    atoms = z_tiles * tile
    shape = jax.ShapeDtypeStruct

    pos = jnp.moveaxis(positions.reshape(3, z_tiles, tile), 0, 1).astype(jnp.bfloat16)
    payload = jnp.concatenate(
        [
            features.reshape(z_tiles, tile, width),
            jnp.pad(pos, ((0, 0), (0, POS_ROWS - 3), (0, 0))),
        ],
        axis=1,
    )
    column = [payload] + [shift(payload, "gz", -step) for step in range(1, sizes[2])]
    south, north = shift(payload, "gy", 1), shift(payload, "gy", -1)
    middle = jnp.stack([south, payload, north])

    mine = lax.dynamic_slice_in_dim(wavevectors, place[2] * waves, waves, axis=1)
    mine = jnp.concatenate([mine, mine], axis=1)
    mine = lax.dynamic_slice_in_dim(mine, place[0] * block, waves, axis=1).astype(jnp.float32)
    fine = jnp.array([1.0 / (count * GRID) for count in counts], jnp.float32)[:, None]
    coarse = jnp.array([1.0 / count for count in counts], jnp.float32)[:, None]
    mine = jnp.concatenate([mine * fine, mine * coarse], axis=0)
    mine = jnp.pad(mine, ((0, POS_ROWS - 6), (0, 0))).astype(jnp.bfloat16)

    table, *parts = call(
        functools.partial(table_kernel, n_blocks, z_tiles),
        [shape((2 * waves, sizes[2] * atoms), jnp.bfloat16)]
        + [shape((2 * block, width), jnp.bfloat16)] * n_blocks,
        place,
        mine,
        charge_weight,
        *column,
        scalars=1,
        name="tables",
    )
    arrived = [parts[0]] + [shift(parts[n], "gx", n) for n in range(1, n_blocks)]
    west, east = shift(middle, "gx", 1), shift(middle, "gx", -1)
    line = call(add_kernel, shape((2 * block, width), jnp.bfloat16), *arrived, name="add_line")
    lines = [line] + [shift(line, "gy", n) for n in range(1, sizes[1])]

    ring = [(dx, dy) for dx in (-1, 0, 1) for dy in (-1, 0, 1)]
    targets = z_tiles + 2
    before, after = column[-1], column[1 % sizes[2]]

    def messages(sources, offsets, extra, name):
        n_columns = sum(len(o) for o in offsets)
        extras = [] if extra is None else [extra]
        return call(
            functools.partial(radial_kernel, offsets, z_tiles, extra is not None),
            shape((targets, tile, width), jnp.float32),
            payload,
            before,
            after,
            *sources,
            radial_mix,
            *extras,
            scratch=[
                pltpu.VMEM((2, NRBF * tile, n_columns * tile), jnp.bfloat16),
                pltpu.VMEM((z_tiles, n_columns * tile, width), jnp.bfloat16),
            ],
            name=name,
        )

    message = messages([middle], [ring[3:6]], None, "radial_near")
    scale = 1.0 / math.sqrt(atoms * sizes[0] * sizes[1] * sizes[2])
    spot = (place[2] * n_blocks + place[0]).reshape(1)
    filtered = call(
        functools.partial(mix_kernel, scale),
        shape((2 * block, width), jnp.bfloat16),
        spot,
        filters,
        mix_weight,
        *lines,
        scalars=1,
        blocks={0: pl.BlockSpec((block, width), lambda i, s: (s[0], 0))},
        name="mix",
    )
    blocks = [filtered] + [shift(filtered, "gx", -n) for n in range(1, n_blocks)]
    message = messages([west, east], [ring[:3], ring[6:]], message, "radial_far")
    sums = call(
        functools.partial(long_kernel, z_tiles, n_blocks),
        [shape((atoms, width), jnp.float32)] * sizes[2],
        table,
        message,
        *blocks,
        name="longrange",
    )
    sums = [sums[0]] + [shift(sums[step], "gz", step) for step in range(1, sizes[2])]
    updated = call(
        node_kernel,
        shape((atoms, width), jnp.bfloat16),
        features.reshape(atoms, width),
        norm_gain.reshape(1, width),
        up_weight,
        down_weight,
        *sums,
        name="node",
    )
    return updated.reshape(features.shape)


def fits(mesh, features, wavevectors):
    count_x, count_y, count_z, tile, width = features
    per = mesh.shape["gx"] * mesh.shape["gz"]
    lengths = [n * GRID for n in (count_x, count_y, count_z)]
    return (
        count_x == mesh.shape["gx"]
        and count_y == mesh.shape["gy"]
        and tile == 128
        and width == 128
        and wavevectors[1] % (16 * per) == 0
        and all(n & (n - 1) == 0 and n <= 2**14 for n in lengths)
    )


def solution(mesh):
    in_specs = (
        P("gx", "gy", "gz", None, None),
        P(None, "gx", "gy", "gz", None),
        P(),
        P(),
        P(),
        P(),
        P(),
        P(),
        P(),
        P(),
    )
    out_specs = P("gx", "gy", "gz", None, None)

    def layer(*args):
        body = fast_device if fits(mesh, args[0].shape, args[2].shape) else on_device
        return jax.shard_map(
            body, mesh=mesh, in_specs=in_specs, out_specs=out_specs, check_vma=False
        )(*args)

    return layer
```

```python
import functools
import math

import jax
import jax.numpy as jnp
import numpy as np
from jax import lax
from jax.experimental import pallas as pl
from jax.experimental.pallas import tpu as pltpu
from jax.sharding import PartitionSpec as P

NRBF = 6
GRID = 64


SHARP = 18.0
TWO_PI = 2.0 * math.pi
EPS = 1e-06
CONTRACT_FIRST = (((0,), (0,)), ((), ()))


def extended(array, sides, width):
    for axis, dim in sides:
        size, length = (lax.axis_size(axis), array.shape[dim])
        up = [(i, (i + 1) % size) for i in range(size)]
        down = [(j, i) for i, j in up]
        last = lax.slice_in_dim(array, length - width, length, axis=dim)
        first = lax.slice_in_dim(array, 0, width, axis=dim)
        before = lax.ppermute(last, axis, up)
        after = lax.ppermute(first, axis, down)
        array = jnp.concatenate([before, array, after], axis=dim)
    return array


def radial_basis(center, nearby_pos):
    tile_size = center.shape[1]
    offsets = (
        jnp.stack(
            [lax.broadcasted_iota(jnp.int32, (3, 3, 3, 1), component) for component in range(3)]
        )
        - 1
    )
    coords = (nearby_pos + offsets * GRID).reshape(3, 27 * tile_size)
    displace = coords[:, None, :] - center[:, :, None]
    square = jnp.sum(displace * displace, axis=0)
    scaled_dist = jnp.sqrt(square.astype(jnp.float32)) / GRID
    inside = (square > 0) & (square < GRID * GRID)
    envelope = jnp.where(inside, (1.0 - scaled_dist * scaled_dist) ** 2, 0.0)
    centres = (jnp.arange(NRBF, dtype=jnp.float32) + 0.5) / NRBF
    radial = (
        jnp.exp(-SHARP * (scaled_dist[:, None, :] - centres[None, :, None]) ** 2)
        * envelope[:, None, :]
    )
    return radial.astype(jnp.bfloat16)


def phase_tables(wavevectors, coords, lengths):
    fraction = jnp.zeros((wavevectors.shape[1], coords.shape[1]), jnp.float32)
    for component in range(3):
        product = jnp.mod(
            wavevectors[component][:, None] * coords[component][None, :], lengths[component]
        )
        fraction = fraction + product.astype(jnp.float32) / lengths[component]
    phase_angle = TWO_PI * fraction
    return (jnp.cos(phase_angle).astype(jnp.bfloat16), jnp.sin(phase_angle).astype(jnp.bfloat16))


def filter_mix(filters, factor, mix_weight):
    return jnp.dot(filters * factor, mix_weight, precision=lax.Precision.HIGHEST).astype(
        jnp.bfloat16
    )


def on_device(
    features,
    positions,
    wavevectors,
    radial_mix,
    charge_weight,
    filters,
    mix_weight,
    norm_gain,
    up_weight,
    down_weight,
):
    count_x, count_y, count_z, tile_size, feat_width = features.shape
    beside_all = extended(features, (("gx", 0), ("gy", 1), ("gz", 2)), 1)
    around_pos = extended(positions, (("gx", 1), ("gy", 2), ("gz", 3)), 1)
    anchor = jnp.zeros((), jnp.int32)

    def one_tile(flat_index):
        tile_x = flat_index // (count_y * count_z)
        tile_y = flat_index // count_z % count_y
        tile_z = flat_index % count_z
        neighbour = lax.dynamic_slice(
            beside_all, (tile_x, tile_y, tile_z, anchor, anchor), (3, 3, 3, tile_size, feat_width)
        )
        nearby_pos = lax.dynamic_slice(
            around_pos, (anchor, tile_x, tile_y, tile_z, anchor), (3, 3, 3, 3, tile_size)
        )
        center = lax.dynamic_slice(
            positions, (anchor, tile_x, tile_y, tile_z, anchor), (3, 1, 1, 1, tile_size)
        ).reshape(3, tile_size)
        radial = radial_basis(center, nearby_pos)
        pooled = jnp.einsum(
            "irj,jd->ird",
            radial,
            neighbour.reshape(27 * tile_size, feat_width),
            preferred_element_type=jnp.float32,
        )
        pooled = pooled.astype(jnp.bfloat16).reshape(tile_size, -1)
        return jnp.dot(pooled, radial_mix, preferred_element_type=jnp.float32)

    message = lax.map(one_tile, jnp.arange(count_x * count_y * count_z, dtype=jnp.int32))
    message = message.reshape(count_x * count_y * count_z * tile_size, feat_width)
    atom_count = count_x * count_y * count_z * tile_size
    counts = (count_x, count_y, count_z)
    axis_sizes = (lax.axis_size("gx"), lax.axis_size("gy"), lax.axis_size("gz"))
    axis_index = (lax.axis_index("gx"), lax.axis_index("gy"), lax.axis_index("gz"))
    lengths = tuple((counts[component] * axis_sizes[component] * GRID for component in range(3)))
    coords = jnp.stack(
        [
            (
                axis_index[component] * counts[component]
                + lax.broadcasted_iota(jnp.int32, (count_x, count_y, count_z, tile_size), component)
            )
            * GRID
            + positions[component]
            for component in range(3)
        ]
    ).reshape(3, atom_count)
    cos_table, sin_table = phase_tables(wavevectors, coords, lengths)
    charges = jnp.dot(
        features.reshape(atom_count, feat_width), charge_weight, preferred_element_type=jnp.float32
    ).astype(jnp.bfloat16)
    partial_cos = jnp.dot(cos_table, charges, preferred_element_type=jnp.float32)
    partial_sin = jnp.dot(sin_table, charges, preferred_element_type=jnp.float32)
    scale = 1.0 / math.sqrt(atom_count * axis_sizes[0] * axis_sizes[1] * axis_sizes[2])
    summed_cos, summed_sin = lax.psum((partial_cos, partial_sin), ("gx", "gy", "gz"))
    filtered_cos = filter_mix(filters, summed_cos * scale, mix_weight)
    filtered_sin = filter_mix(filters, summed_sin * scale, mix_weight)
    longrange = lax.dot_general(
        cos_table, filtered_cos, CONTRACT_FIRST, preferred_element_type=jnp.float32
    )
    longrange = longrange + lax.dot_general(
        sin_table, filtered_sin, CONTRACT_FIRST, preferred_element_type=jnp.float32
    )
    flat_sum = features.reshape(atom_count, feat_width).astype(jnp.float32) + message + longrange
    normed = (
        flat_sum
        * lax.rsqrt(jnp.mean(flat_sum * flat_sum, axis=-1, keepdims=True) + EPS)
        * norm_gain
    )
    hidden = jax.nn.silu(
        jnp.dot(normed.astype(jnp.bfloat16), up_weight, preferred_element_type=jnp.float32)
    ).astype(jnp.bfloat16)
    updated = flat_sum + jnp.dot(hidden, down_weight, preferred_element_type=jnp.float32)
    return updated.reshape(features.shape).astype(jnp.bfloat16)


LOG2E = 1.4426950408889634
POS_ROWS = 16
ROUND = 12582912.0


def shift(array, axis, step):
    size = lax.axis_size(axis)
    return lax.ppermute(array, axis, [(i, (i + step) % size) for i in range(size)])


def sin_coefficients():
    nodes = np.cos((np.arange(400) + 0.5) / 400 * np.pi) * 0.25
    powers = np.stack([nodes ** (2 * n + 1) for n in range(6)], axis=1)
    scale = np.abs(powers).max(axis=0)
    fit = np.linalg.lstsq(powers / scale, np.sin(2 * np.pi * nodes), rcond=None)[0] / scale
    return [float(value) for value in fit]


SIN_FIT = sin_coefficients()


def sin_turns(u):
    square = u * u
    value = square * SIN_FIT[-1] + SIN_FIT[-2]
    for coefficient in SIN_FIT[-3::-1]:
        value = value * square + coefficient
    return value * u


def from_nearest(turns):
    return turns - ((turns + ROUND) - ROUND)


def table_kernel(n_blocks, z_tiles, place_ref, waves_ref, charge_ref, *refs):
    z_size = len(refs) - 1 - n_blocks
    columns, table_ref, parts = refs[:z_size], refs[z_size], refs[z_size + 1 :]
    tile = columns[0].shape[2]
    block = waves_ref.shape[1] // n_blocks
    row = lax.broadcasted_iota(jnp.int32, (POS_ROWS, tile), 0)
    coords, charges = [], []
    for step in range(z_size):
        for t in range(z_tiles):
            pos = columns[step][t, tile : tile + POS_ROWS, :].astype(jnp.float32)
            z = lax.rem(place_ref[2] + step, z_size) * z_tiles + t
            pos = jnp.where(row == 3, place_ref[0].astype(jnp.float32), pos)
            pos = jnp.where(row == 4, place_ref[1].astype(jnp.float32), pos)
            pos = jnp.where(row == 5, z.astype(jnp.float32), pos)
            coords.append(pos.astype(jnp.bfloat16))
            charges.append(
                jnp.dot(
                    columns[step][t, :tile, :], charge_ref[...], preferred_element_type=jnp.float32
                ).astype(jnp.bfloat16)
            )
    coords = jnp.concatenate(coords, axis=1)
    charges = jnp.concatenate(charges, axis=0)
    for n in range(n_blocks):
        turns = lax.dot_general(
            waves_ref[:, n * block : (n + 1) * block],
            coords,
            CONTRACT_FIRST,
            preferred_element_type=jnp.float32,
        )
        cos_part = sin_turns(0.25 - jnp.abs(from_nearest(turns)))
        sin_part = sin_turns(0.25 - jnp.abs(from_nearest(turns - 0.25)))
        base = 2 * n * block
        table_ref[base : base + block, :] = cos_part.astype(jnp.bfloat16)
        table_ref[base + block : base + 2 * block, :] = sin_part.astype(jnp.bfloat16)
        parts[n][...] = jnp.dot(
            table_ref[base : base + 2 * block, :], charges, preferred_element_type=jnp.float32
        ).astype(jnp.bfloat16)


def add_kernel(*refs):
    total = refs[0][...].astype(jnp.float32)
    for ref in refs[1:-1]:
        total = total + ref[...].astype(jnp.float32)
    refs[-1][...] = total.astype(refs[-1].dtype)


def mix_kernel(scale, filters_ref, mix_ref, *refs):
    total = refs[0][...].astype(jnp.float32)
    for ref in refs[1:-1]:
        total = total + ref[...].astype(jnp.float32)
    both = jnp.concatenate([filters_ref[...], filters_ref[...]], axis=0)
    refs[-1][...] = jnp.dot(
        both * (total * scale),
        mix_ref[...],
        precision=lax.Precision.HIGHEST,
        preferred_element_type=jnp.float32,
    ).astype(jnp.bfloat16)


def rows_of(row, values):
    out = jnp.zeros(row.shape, jnp.float32)
    for n, value in enumerate(values):
        out = jnp.where(row == n, value, out)
    return out.astype(jnp.bfloat16)


def split_norm(x, y, z):
    norm = x * x + y * y + z * z
    high = jnp.floor(norm * 16.0) * 0.0625
    return high, norm - high


def radial_kernel(offsets, z_tiles, has_extra, *refs):
    own_ref, before_ref, after_ref = refs[:3]
    groups = refs[3 : 3 + len(offsets)]
    mix_ref = refs[3 + len(offsets)]
    extra_ref = refs[4 + len(offsets)] if has_extra else None
    out_ref, radial_ref, feature_ref = refs[-3:]
    tile = own_ref.shape[2]
    row = lax.broadcasted_iota(jnp.int32, (POS_ROWS, tile), 0)
    columns = [(g, c, dx, dy) for g, per in enumerate(offsets) for c, (dx, dy) in enumerate(per)]

    def unit(ref_rows):
        pos = ref_rows.astype(jnp.float32) * (1.0 / GRID)
        return pos[0:1, :], pos[1:2, :], pos[2:3, :]

    sources = {}
    for slot, (g, c, dx, dy) in enumerate(columns):
        for sz in range(z_tiles):
            x, y, z = unit(groups[g][c, sz, tile : tile + POS_ROWS, :])
            high, low = split_norm(x, y, z)
            one = jnp.ones_like(x)
            sources[slot, sz] = rows_of(row, [x, y, z, one, one, high, low])
            feature_ref[sz, slot * tile : (slot + 1) * tile, :] = groups[g][c, sz, :tile, :]
    targets = [(-1, before_ref, z_tiles - 1)]
    targets += [(t, own_ref, t) for t in range(z_tiles)]
    targets += [(z_tiles, after_ref, 0)]
    for index, (tz, ref, at) in enumerate(targets):
        x0, y0, z0 = unit(ref[at, tile : tile + POS_ROWS, :])
        near = [sz for sz in range(z_tiles) if abs(sz - tz) <= 1]
        pooled = [None] * NRBF
        for place, sz in enumerate(near):
            buffer = radial_ref.at[(index + place) % 2]
            for slot, (g, c, dx, dy) in enumerate(columns):
                x, y, z = x0 - dx, y0 - dy, z0 - (sz - tz)
                high, low = split_norm(x, y, z)
                one = jnp.ones_like(x)
                target = rows_of(row, [-2 * x, -2 * y, -2 * z, high, low, one, one])
                square = lax.dot_general(
                    target, sources[slot, sz], CONTRACT_FIRST, preferred_element_type=jnp.float32
                )
                square = jnp.where(square == 0.0, 1.0, jnp.minimum(square, 1.0))
                dist = square * lax.rsqrt(square)
                lack = 1.0 - square
                value = jnp.exp2(dist * (3.0 * LOG2E - (SHARP * LOG2E) * dist)) * (lack * lack)
                growth = jnp.exp2(dist * (6.0 * LOG2E))
                for r in range(NRBF):
                    buffer[r * tile : (r + 1) * tile, slot * tile : (slot + 1) * tile] = (
                        value.astype(jnp.bfloat16)
                    )
                    if r + 1 < NRBF:
                        value = value * growth
            part = jnp.dot(buffer[...], feature_ref[sz], preferred_element_type=jnp.float32)
            for r in range(NRBF):
                piece = part[r * tile : (r + 1) * tile, :]
                pooled[r] = piece if pooled[r] is None else pooled[r] + piece
        message = extra_ref[index] if has_extra else None
        for r in range(NRBF):
            level = math.exp(-SHARP * ((r + 0.5) / NRBF) ** 2)
            part = jnp.dot(
                (pooled[r] * level).astype(jnp.bfloat16),
                mix_ref[r * tile : (r + 1) * tile, :],
                preferred_element_type=jnp.float32,
            )
            message = part if message is None else message + part
        out_ref[index] = message


def long_kernel(z_tiles, n_blocks, table_ref, message_ref, *refs):
    blocks, outs = refs[:n_blocks], refs[n_blocks:]
    z_size, tile = len(outs), message_ref.shape[1]
    filtered = jnp.concatenate([ref[...] for ref in blocks], axis=0)
    flipped = lax.dot_general(
        filtered, table_ref[...], CONTRACT_FIRST, preferred_element_type=jnp.float32
    )
    for step in range(z_size):
        for t in range(z_tiles):
            at = (step * z_tiles + t) * tile
            value = flipped[:, at : at + tile].T
            if step == 0:
                value = value + message_ref[1 + t]
            if step == (z_size - 1) % z_size and t == z_tiles - 1:
                value = value + message_ref[0]
            if step == 1 % z_size and t == 0:
                value = value + message_ref[z_tiles + 1]
            outs[step][t * tile : (t + 1) * tile, :] = value


def node_kernel(features_ref, gain_ref, up_ref, down_ref, *refs):
    total = features_ref[...].astype(jnp.float32)
    for ref in refs[:-1]:
        total = total + ref[...]
    normed = (
        total
        * lax.rsqrt(jnp.mean(total * total, axis=-1, keepdims=True) + EPS)
        * gain_ref[...]
    )
    inner = jnp.dot(normed.astype(jnp.bfloat16), up_ref[...], preferred_element_type=jnp.float32)
    hidden = (inner / (1.0 + jnp.exp(-inner))).astype(jnp.bfloat16)
    updated = total + jnp.dot(hidden, down_ref[...], preferred_element_type=jnp.float32)
    refs[-1][...] = updated.astype(jnp.bfloat16)


def call(kernel, out_shape, *args, scalars=0, scratch=(), name=None):
    in_vmem = pl.BlockSpec(memory_space=pltpu.VMEM)
    held = [pltpu.with_memory_space_constraint(a, pltpu.VMEM) for a in args[scalars:]]
    args = list(args[:scalars]) + held
    specs = [pl.BlockSpec(memory_space=pltpu.SMEM)] * scalars
    single = not isinstance(out_shape, (list, tuple))
    return pl.pallas_call(
        kernel,
        out_shape=jax.tree.map(lambda o: pltpu.VMEM(o.shape, o.dtype), out_shape),
        in_specs=specs + [in_vmem] * (len(args) - scalars),
        out_specs=in_vmem if single else [in_vmem] * len(out_shape),
        scratch_shapes=list(scratch),
        name=name,
    )(*args)


def fast_device(
    features,
    positions,
    wavevectors,
    radial_mix,
    charge_weight,
    filters,
    mix_weight,
    norm_gain,
    up_weight,
    down_weight,
):
    z_tiles, tile, width = features.shape[2:]
    sizes = tuple(lax.axis_size(axis) for axis in ("gx", "gy", "gz"))
    place = jnp.stack([lax.axis_index(axis) for axis in ("gx", "gy", "gz")]).astype(jnp.int32)
    counts = (sizes[0], sizes[1], sizes[2] * z_tiles)
    n_blocks, waves = sizes[0], wavevectors.shape[1] // sizes[2]
    block = waves // n_blocks
    atoms = z_tiles * tile
    shape = jax.ShapeDtypeStruct

    pos = jnp.moveaxis(positions.reshape(3, z_tiles, tile), 0, 1).astype(jnp.bfloat16)
    payload = jnp.concatenate(
        [
            features.reshape(z_tiles, tile, width),
            jnp.pad(pos, ((0, 0), (0, POS_ROWS - 3), (0, 0))),
        ],
        axis=1,
    )
    column = [payload] + [shift(payload, "gz", -step) for step in range(1, sizes[2])]
    south, north = shift(payload, "gy", 1), shift(payload, "gy", -1)
    middle = jnp.stack([south, payload, north])

    mine = lax.dynamic_slice_in_dim(wavevectors, place[2] * waves, waves, axis=1)
    mine = jnp.concatenate([mine, mine], axis=1)
    mine = lax.dynamic_slice_in_dim(mine, place[0] * block, waves, axis=1).astype(jnp.float32)
    fine = jnp.array([1.0 / (count * GRID) for count in counts], jnp.float32)[:, None]
    coarse = jnp.array([1.0 / count for count in counts], jnp.float32)[:, None]
    mine = jnp.concatenate([mine * fine, mine * coarse], axis=0)
    mine = jnp.pad(mine, ((0, POS_ROWS - 6), (0, 0))).astype(jnp.bfloat16)

    table, *parts = call(
        functools.partial(table_kernel, n_blocks, z_tiles),
        [shape((2 * waves, sizes[2] * atoms), jnp.bfloat16)]
        + [shape((2 * block, width), jnp.bfloat16)] * n_blocks,
        place,
        mine,
        charge_weight,
        *column,
        scalars=1,
        name="tables",
    )
    arrived = [parts[0]] + [shift(parts[n], "gx", n) for n in range(1, n_blocks)]
    west, east = shift(middle, "gx", 1), shift(middle, "gx", -1)
    line = call(add_kernel, shape((2 * block, width), jnp.bfloat16), *arrived, name="add_line")
    lines = [line] + [shift(line, "gy", n) for n in range(1, sizes[1])]

    ring = [(dx, dy) for dx in (-1, 0, 1) for dy in (-1, 0, 1)]
    targets = z_tiles + 2
    before, after = column[-1], column[1 % sizes[2]]

    def messages(sources, offsets, extra, name):
        n_columns = sum(len(o) for o in offsets)
        extras = [] if extra is None else [extra]
        return call(
            functools.partial(radial_kernel, offsets, z_tiles, extra is not None),
            shape((targets, tile, width), jnp.float32),
            payload,
            before,
            after,
            *sources,
            radial_mix,
            *extras,
            scratch=[
                pltpu.VMEM((2, NRBF * tile, n_columns * tile), jnp.bfloat16),
                pltpu.VMEM((z_tiles, n_columns * tile, width), jnp.bfloat16),
            ],
            name=name,
        )

    message = messages([middle], [ring[3:6]], None, "radial_near")
    scale = 1.0 / math.sqrt(atoms * sizes[0] * sizes[1] * sizes[2])
    spot = place[2] * waves + place[0] * block
    mine_filters = lax.dynamic_slice_in_dim(filters, spot, block, axis=0)
    filtered = call(
        functools.partial(mix_kernel, scale),
        shape((2 * block, width), jnp.bfloat16),
        mine_filters,
        mix_weight,
        *lines,
        name="mix",
    )
    blocks = [filtered] + [shift(filtered, "gx", -n) for n in range(1, n_blocks)]
    message = messages([west, east], [ring[:3], ring[6:]], message, "radial_far")
    sums = call(
        functools.partial(long_kernel, z_tiles, n_blocks),
        [shape((atoms, width), jnp.float32)] * sizes[2],
        table,
        message,
        *blocks,
        name="longrange",
    )
    sums = [sums[0]] + [shift(sums[step], "gz", step) for step in range(1, sizes[2])]
    updated = call(
        node_kernel,
        shape((atoms, width), jnp.bfloat16),
        features.reshape(atoms, width),
        norm_gain.reshape(1, width),
        up_weight,
        down_weight,
        *sums,
        name="node",
    )
    return updated.reshape(features.shape)


def fits(mesh, features, wavevectors):
    count_x, count_y, count_z, tile, width = features
    per = mesh.shape["gx"] * mesh.shape["gz"]
    lengths = [n * GRID for n in (count_x, count_y, count_z)]
    return (
        count_x == mesh.shape["gx"]
        and count_y == mesh.shape["gy"]
        and tile == 128
        and width == 128
        and wavevectors[1] % (16 * per) == 0
        and all(n & (n - 1) == 0 and n <= 2**14 for n in lengths)
    )


def solution(mesh):
    in_specs = (
        P("gx", "gy", "gz", None, None),
        P(None, "gx", "gy", "gz", None),
        P(),
        P(),
        P(),
        P(),
        P(),
        P(),
        P(),
        P(),
    )
    out_specs = P("gx", "gy", "gz", None, None)

    def layer(*args):
        body = fast_device if fits(mesh, args[0].shape, args[2].shape) else on_device
        return jax.shard_map(
            body, mesh=mesh, in_specs=in_specs, out_specs=out_specs, check_vma=False
        )(*args)

    return layer
```

```python
import functools
import math

import jax
import jax.numpy as jnp
import numpy as np
from jax import lax
from jax.experimental import pallas as pl
from jax.experimental.pallas import tpu as pltpu
from jax.sharding import PartitionSpec as P

NRBF = 6
GRID = 64


SHARP = 18.0
TWO_PI = 2.0 * math.pi
EPS = 1e-06
CONTRACT_FIRST = (((0,), (0,)), ((), ()))


def extended(array, sides, width):
    for axis, dim in sides:
        size, length = (lax.axis_size(axis), array.shape[dim])
        up = [(i, (i + 1) % size) for i in range(size)]
        down = [(j, i) for i, j in up]
        last = lax.slice_in_dim(array, length - width, length, axis=dim)
        first = lax.slice_in_dim(array, 0, width, axis=dim)
        before = lax.ppermute(last, axis, up)
        after = lax.ppermute(first, axis, down)
        array = jnp.concatenate([before, array, after], axis=dim)
    return array


def radial_basis(center, nearby_pos):
    tile_size = center.shape[1]
    offsets = (
        jnp.stack(
            [lax.broadcasted_iota(jnp.int32, (3, 3, 3, 1), component) for component in range(3)]
        )
        - 1
    )
    coords = (nearby_pos + offsets * GRID).reshape(3, 27 * tile_size)
    displace = coords[:, None, :] - center[:, :, None]
    square = jnp.sum(displace * displace, axis=0)
    scaled_dist = jnp.sqrt(square.astype(jnp.float32)) / GRID
    inside = (square > 0) & (square < GRID * GRID)
    envelope = jnp.where(inside, (1.0 - scaled_dist * scaled_dist) ** 2, 0.0)
    centres = (jnp.arange(NRBF, dtype=jnp.float32) + 0.5) / NRBF
    radial = (
        jnp.exp(-SHARP * (scaled_dist[:, None, :] - centres[None, :, None]) ** 2)
        * envelope[:, None, :]
    )
    return radial.astype(jnp.bfloat16)


def phase_tables(wavevectors, coords, lengths):
    fraction = jnp.zeros((wavevectors.shape[1], coords.shape[1]), jnp.float32)
    for component in range(3):
        product = jnp.mod(
            wavevectors[component][:, None] * coords[component][None, :], lengths[component]
        )
        fraction = fraction + product.astype(jnp.float32) / lengths[component]
    phase_angle = TWO_PI * fraction
    return (jnp.cos(phase_angle).astype(jnp.bfloat16), jnp.sin(phase_angle).astype(jnp.bfloat16))


def filter_mix(filters, factor, mix_weight):
    return jnp.dot(filters * factor, mix_weight, precision=lax.Precision.HIGHEST).astype(
        jnp.bfloat16
    )


def on_device(
    features,
    positions,
    wavevectors,
    radial_mix,
    charge_weight,
    filters,
    mix_weight,
    norm_gain,
    up_weight,
    down_weight,
):
    count_x, count_y, count_z, tile_size, feat_width = features.shape
    beside_all = extended(features, (("gx", 0), ("gy", 1), ("gz", 2)), 1)
    around_pos = extended(positions, (("gx", 1), ("gy", 2), ("gz", 3)), 1)
    anchor = jnp.zeros((), jnp.int32)

    def one_tile(flat_index):
        tile_x = flat_index // (count_y * count_z)
        tile_y = flat_index // count_z % count_y
        tile_z = flat_index % count_z
        neighbour = lax.dynamic_slice(
            beside_all, (tile_x, tile_y, tile_z, anchor, anchor), (3, 3, 3, tile_size, feat_width)
        )
        nearby_pos = lax.dynamic_slice(
            around_pos, (anchor, tile_x, tile_y, tile_z, anchor), (3, 3, 3, 3, tile_size)
        )
        center = lax.dynamic_slice(
            positions, (anchor, tile_x, tile_y, tile_z, anchor), (3, 1, 1, 1, tile_size)
        ).reshape(3, tile_size)
        radial = radial_basis(center, nearby_pos)
        pooled = jnp.einsum(
            "irj,jd->ird",
            radial,
            neighbour.reshape(27 * tile_size, feat_width),
            preferred_element_type=jnp.float32,
        )
        pooled = pooled.astype(jnp.bfloat16).reshape(tile_size, -1)
        return jnp.dot(pooled, radial_mix, preferred_element_type=jnp.float32)

    message = lax.map(one_tile, jnp.arange(count_x * count_y * count_z, dtype=jnp.int32))
    message = message.reshape(count_x * count_y * count_z * tile_size, feat_width)
    atom_count = count_x * count_y * count_z * tile_size
    counts = (count_x, count_y, count_z)
    axis_sizes = (lax.axis_size("gx"), lax.axis_size("gy"), lax.axis_size("gz"))
    axis_index = (lax.axis_index("gx"), lax.axis_index("gy"), lax.axis_index("gz"))
    lengths = tuple((counts[component] * axis_sizes[component] * GRID for component in range(3)))
    coords = jnp.stack(
        [
            (
                axis_index[component] * counts[component]
                + lax.broadcasted_iota(jnp.int32, (count_x, count_y, count_z, tile_size), component)
            )
            * GRID
            + positions[component]
            for component in range(3)
        ]
    ).reshape(3, atom_count)
    cos_table, sin_table = phase_tables(wavevectors, coords, lengths)
    charges = jnp.dot(
        features.reshape(atom_count, feat_width), charge_weight, preferred_element_type=jnp.float32
    ).astype(jnp.bfloat16)
    partial_cos = jnp.dot(cos_table, charges, preferred_element_type=jnp.float32)
    partial_sin = jnp.dot(sin_table, charges, preferred_element_type=jnp.float32)
    scale = 1.0 / math.sqrt(atom_count * axis_sizes[0] * axis_sizes[1] * axis_sizes[2])
    summed_cos, summed_sin = lax.psum((partial_cos, partial_sin), ("gx", "gy", "gz"))
    filtered_cos = filter_mix(filters, summed_cos * scale, mix_weight)
    filtered_sin = filter_mix(filters, summed_sin * scale, mix_weight)
    longrange = lax.dot_general(
        cos_table, filtered_cos, CONTRACT_FIRST, preferred_element_type=jnp.float32
    )
    longrange = longrange + lax.dot_general(
        sin_table, filtered_sin, CONTRACT_FIRST, preferred_element_type=jnp.float32
    )
    flat_sum = features.reshape(atom_count, feat_width).astype(jnp.float32) + message + longrange
    normed = (
        flat_sum
        * lax.rsqrt(jnp.mean(flat_sum * flat_sum, axis=-1, keepdims=True) + EPS)
        * norm_gain
    )
    hidden = jax.nn.silu(
        jnp.dot(normed.astype(jnp.bfloat16), up_weight, preferred_element_type=jnp.float32)
    ).astype(jnp.bfloat16)
    updated = flat_sum + jnp.dot(hidden, down_weight, preferred_element_type=jnp.float32)
    return updated.reshape(features.shape).astype(jnp.bfloat16)


LOG2E = 1.4426950408889634
POS_ROWS = 16
ROUND = 12582912.0
PIECE = 2
VMEM_GRANT = 16 * 2**20


def shift(array, axis, step):
    size = lax.axis_size(axis)
    return lax.ppermute(array, axis, [(i, (i + step) % size) for i in range(size)])


def sin_coefficients():
    nodes = np.cos((np.arange(400) + 0.5) / 400 * np.pi) * 0.25
    powers = np.stack([nodes ** (2 * n + 1) for n in range(5)], axis=1)
    scale = np.abs(powers).max(axis=0)
    fit = np.linalg.lstsq(powers / scale, np.sin(2 * np.pi * nodes), rcond=None)[0] / scale
    return [float(value) for value in fit]


SIN_FIT = sin_coefficients()


def sin_turns(u):
    square = u * u
    value = square * SIN_FIT[-1] + SIN_FIT[-2]
    for coefficient in SIN_FIT[-3::-1]:
        value = value * square + coefficient
    return value * u


def from_nearest(turns):
    return turns - ((turns + ROUND) - ROUND)


def table_kernel(n_blocks, z_tiles, place_ref, waves_ref, charge_ref, *refs):
    z_size = len(refs) - 2 - n_blocks
    columns, copy_ref, table_ref, parts = refs[:z_size], *refs[z_size : z_size + 2], refs[z_size + 2 :]
    copy_ref[...] = columns[0][...]
    tile = columns[0].shape[2]
    block = waves_ref.shape[1] // n_blocks
    row = lax.broadcasted_iota(jnp.int32, (POS_ROWS, tile), 0)
    coords, charges = [], []
    for step in range(z_size):
        for t in range(z_tiles):
            pos = columns[step][t, tile : tile + POS_ROWS, :].astype(jnp.float32)
            z = lax.rem(place_ref[2] + step, z_size) * z_tiles + t
            pos = jnp.where(row == 3, place_ref[0].astype(jnp.float32), pos)
            pos = jnp.where(row == 4, place_ref[1].astype(jnp.float32), pos)
            pos = jnp.where(row == 5, z.astype(jnp.float32), pos)
            coords.append(pos.astype(jnp.bfloat16))
            charges.append(
                jnp.dot(
                    columns[step][t, :tile, :], charge_ref[...], preferred_element_type=jnp.float32
                ).astype(jnp.bfloat16)
            )
    coords = jnp.concatenate(coords, axis=1)
    charges = jnp.concatenate(charges, axis=0)
    for n in range(n_blocks):
        turns = lax.dot_general(
            waves_ref[:, n * block : (n + 1) * block],
            coords,
            CONTRACT_FIRST,
            preferred_element_type=jnp.float32,
        )
        cos_part = sin_turns(0.25 - jnp.abs(from_nearest(turns)))
        sin_part = sin_turns(0.25 - jnp.abs(from_nearest(turns - 0.25)))
        base = 2 * n * block
        table_ref[base : base + block, :] = cos_part.astype(jnp.bfloat16)
        table_ref[base + block : base + 2 * block, :] = sin_part.astype(jnp.bfloat16)
        parts[n][...] = jnp.dot(
            table_ref[base : base + 2 * block, :], charges, preferred_element_type=jnp.float32
        ).astype(jnp.bfloat16)


def add_kernel(*refs):
    total = refs[0][...].astype(jnp.float32)
    for ref in refs[1:-1]:
        total = total + ref[...].astype(jnp.float32)
    refs[-1][...] = total.astype(refs[-1].dtype)


def mix_kernel(scale, filters_ref, mix_ref, *refs):
    total = refs[0][...].astype(jnp.float32)
    for ref in refs[1:-1]:
        total = total + ref[...].astype(jnp.float32)
    both = jnp.concatenate([filters_ref[...], filters_ref[...]], axis=0)
    refs[-1][...] = jnp.dot(
        both * (total * scale),
        mix_ref[...],
        precision=lax.Precision.HIGHEST,
        preferred_element_type=jnp.float32,
    ).astype(jnp.bfloat16)


def rows_of(row, values):
    out = jnp.zeros(row.shape, jnp.float32)
    for n, value in enumerate(values):
        out = jnp.where(row == n, value, out)
    return out.astype(jnp.bfloat16)


def split_norm(x, y, z):
    norm = x * x + y * y + z * z
    high = jnp.floor(norm * 16.0) * 0.0625
    return high, norm - high


def radial_kernel(offsets, z_tiles, has_extra, *refs):
    own_ref, before_ref, after_ref = refs[:3]
    groups = refs[3 : 3 + len(offsets)]
    mix_ref = refs[3 + len(offsets)]
    extra_ref = refs[4 + len(offsets)] if has_extra else None
    out_ref, radial_ref, feature_ref = refs[-3:]
    tile = own_ref.shape[2]
    row = lax.broadcasted_iota(jnp.int32, (POS_ROWS, tile), 0)
    columns = [(g, c, dx, dy) for g, per in enumerate(offsets) for c, (dx, dy) in enumerate(per)]

    def unit(ref_rows):
        pos = ref_rows.astype(jnp.float32) * (1.0 / GRID)
        return pos[0:1, :], pos[1:2, :], pos[2:3, :]

    sources = {}
    for slot, (g, c, dx, dy) in enumerate(columns):
        for sz in range(z_tiles):
            x, y, z = unit(groups[g][c, sz, tile : tile + POS_ROWS, :])
            high, low = split_norm(x, y, z)
            one = jnp.ones_like(x)
            sources[slot, sz] = rows_of(row, [x, y, z, one, one, high, low])
            feature_ref[sz, slot * tile : (slot + 1) * tile, :] = groups[g][c, sz, :tile, :]
    targets = [(-1, before_ref, z_tiles - 1)]
    targets += [(t, own_ref, t) for t in range(z_tiles)]
    targets += [(z_tiles, after_ref, 0)]
    blocks = [
        (index, sz)
        for index, (tz, ref, at) in enumerate(targets)
        for sz in range(z_tiles)
        if abs(sz - tz) <= 1
    ]
    pooled = {}

    def basis(block_at, slot):
        index, sz = blocks[block_at]
        tz, ref, at = targets[index]
        dx, dy = columns[slot][2:]
        x0, y0, z0 = unit(ref[at, tile : tile + POS_ROWS, :])
        x, y, z = x0 - dx, y0 - dy, z0 - (sz - tz)
        high, low = split_norm(x, y, z)
        one = jnp.ones_like(x)
        target = rows_of(row, [-2 * x, -2 * y, -2 * z, high, low, one, one])
        square = lax.dot_general(
            target, sources[slot, sz], CONTRACT_FIRST, preferred_element_type=jnp.float32
        )
        square = jnp.where(square == 0.0, 1.0, jnp.minimum(square, 1.0))
        dist = square * lax.rsqrt(square)
        lack = 1.0 - square
        value = jnp.exp2(dist * (3.0 * LOG2E - (SHARP * LOG2E) * dist)) * (lack * lack)
        growth = jnp.exp2(dist * (6.0 * LOG2E))
        for r in range(NRBF):
            radial_ref[
                block_at % 2, r * tile : (r + 1) * tile, slot * tile : (slot + 1) * tile
            ] = value.astype(jnp.bfloat16)
            if r + 1 < NRBF:
                value = value * growth

    def pool(block_at, r):
        index, sz = blocks[block_at]
        part = jnp.dot(
            radial_ref[block_at % 2, r * tile : (r + PIECE) * tile, :],
            feature_ref[sz],
            preferred_element_type=jnp.float32,
        )
        for step in range(PIECE):
            piece = part[step * tile : (step + 1) * tile, :]
            key = index, r + step
            pooled[key] = pooled[key] + piece if key in pooled else piece

    def finish(index):
        message = extra_ref[index] if has_extra else None
        for r in range(NRBF):
            level = math.exp(-SHARP * ((r + 0.5) / NRBF) ** 2)
            part = jnp.dot(
                (pooled.pop((index, r)) * level).astype(jnp.bfloat16),
                mix_ref[r * tile : (r + 1) * tile, :],
                preferred_element_type=jnp.float32,
            )
            message = part if message is None else message + part
        out_ref[index] = message

    n_pieces = NRBF // PIECE
    for block_at in range(len(blocks) + 1):
        work = []
        if block_at < len(blocks):
            work += [(slot / len(columns), 0, slot) for slot in range(len(columns))]
        if block_at > 0:
            work += [((n + 0.5) / n_pieces, 1, n) for n in range(n_pieces)]
        for _, kind, n in sorted(work):
            if kind:
                pool(block_at - 1, n * PIECE)
            else:
                basis(block_at, n)
        if block_at > 0:
            index = blocks[block_at - 1][0]
            if block_at == len(blocks) or blocks[block_at][0] != index:
                finish(index)


def long_kernel(z_tiles, n_blocks, table_ref, message_ref, *refs):
    blocks, outs = refs[:n_blocks], refs[n_blocks:]
    z_size, tile = len(outs), message_ref.shape[1]
    filtered = jnp.concatenate([ref[...] for ref in blocks], axis=0)
    flipped = lax.dot_general(
        filtered, table_ref[...], CONTRACT_FIRST, preferred_element_type=jnp.float32
    )
    for step in range(z_size):
        for t in range(z_tiles):
            at = (step * z_tiles + t) * tile
            value = flipped[:, at : at + tile].T
            if step == 0:
                value = value + message_ref[1 + t]
            if step == (z_size - 1) % z_size and t == z_tiles - 1:
                value = value + message_ref[0]
            if step == 1 % z_size and t == 0:
                value = value + message_ref[z_tiles + 1]
            outs[step][t * tile : (t + 1) * tile, :] = value


def node_kernel(features_ref, gain_ref, up_ref, down_ref, *refs):
    total = features_ref[...].astype(jnp.float32)
    for ref in refs[:-1]:
        total = total + ref[...]
    normed = (
        total
        * lax.rsqrt(jnp.mean(total * total, axis=-1, keepdims=True) + EPS)
        * gain_ref[...]
    )
    inner = jnp.dot(normed.astype(jnp.bfloat16), up_ref[...], preferred_element_type=jnp.float32)
    hidden = (inner / (1.0 + jnp.exp(-inner))).astype(jnp.bfloat16)
    updated = total + jnp.dot(hidden, down_ref[...], preferred_element_type=jnp.float32)
    refs[-1][...] = updated.astype(jnp.bfloat16)


def call(kernel, out_shape, *args, scalars=0, after=(), scratch=(), name=None, keep=True):
    in_vmem = pl.BlockSpec(memory_space=pltpu.VMEM)
    anywhere = pl.BlockSpec(memory_space=pl.ANY)
    single = not isinstance(out_shape, (list, tuple))
    held = [pltpu.with_memory_space_constraint(a, pltpu.VMEM) for a in args[scalars:]]
    n_args, n_after = len(args), len(after)
    if keep:
        out_shape = jax.tree.map(lambda o: pltpu.VMEM(o.shape, o.dtype), out_shape)

    def body(*refs):
        kernel(*refs[:n_args], *refs[n_args + n_after :])

    return pl.pallas_call(
        body,
        out_shape=out_shape,
        in_specs=[pl.BlockSpec(memory_space=pltpu.SMEM)] * scalars
        + [in_vmem] * len(held)
        + [anywhere] * n_after,
        out_specs=in_vmem if single else [in_vmem] * len(out_shape),
        scratch_shapes=list(scratch),
        compiler_params=pltpu.CompilerParams(vmem_limit_bytes=VMEM_GRANT),
        name=name,
    )(*args[:scalars], *held, *after)


def fast_device(
    features,
    positions,
    wavevectors,
    radial_mix,
    charge_weight,
    filters,
    mix_weight,
    norm_gain,
    up_weight,
    down_weight,
):
    z_tiles, tile, width = features.shape[2:]
    sizes = tuple(lax.axis_size(axis) for axis in ("gx", "gy", "gz"))
    place = jnp.stack([lax.axis_index(axis) for axis in ("gx", "gy", "gz")]).astype(jnp.int32)
    counts = (sizes[0], sizes[1], sizes[2] * z_tiles)
    n_blocks, waves = sizes[0], wavevectors.shape[1] // sizes[2]
    block = waves // n_blocks
    atoms = z_tiles * tile
    shape = jax.ShapeDtypeStruct

    pos = jnp.moveaxis(positions.reshape(3, z_tiles, tile), 0, 1).astype(jnp.bfloat16)
    payload = jnp.concatenate(
        [
            features.reshape(z_tiles, tile, width),
            jnp.pad(pos, ((0, 0), (0, POS_ROWS - 3), (0, 0))),
        ],
        axis=1,
    )
    column = [payload] + [shift(payload, "gz", -step) for step in range(1, sizes[2])]
    mine = lax.dynamic_slice_in_dim(wavevectors, place[2] * waves, waves, axis=1)
    mine = jnp.concatenate([mine, mine], axis=1)
    mine = lax.dynamic_slice_in_dim(mine, place[0] * block, waves, axis=1).astype(jnp.float32)
    fine = jnp.array([1.0 / (count * GRID) for count in counts], jnp.float32)[:, None]
    coarse = jnp.array([1.0 / count for count in counts], jnp.float32)[:, None]
    mine = jnp.concatenate([mine * fine, mine * coarse], axis=0)
    mine = jnp.pad(mine, ((0, POS_ROWS - 6), (0, 0))).astype(jnp.bfloat16)

    later, table, *parts = call(
        functools.partial(table_kernel, n_blocks, z_tiles),
        [shape(payload.shape, payload.dtype), shape((2 * waves, sizes[2] * atoms), jnp.bfloat16)]
        + [shape((2 * block, width), jnp.bfloat16)] * n_blocks,
        place,
        mine,
        charge_weight,
        *column,
        scalars=1,
        name="tables",
    )
    south, north = shift(later, "gy", 1), shift(later, "gy", -1)
    middle = jnp.stack([south, later, north])
    arrived = [parts[0]] + [shift(parts[n], "gx", n) for n in range(1, n_blocks)]
    west, east = shift(middle, "gx", 1), shift(middle, "gx", -1)
    line = call(add_kernel, shape((2 * block, width), jnp.bfloat16), *arrived, name="add_line")
    lines = [line] + [shift(line, "gy", n) for n in range(1, sizes[1])]

    ring = [(dx, dy) for dx in (-1, 0, 1) for dy in (-1, 0, 1)]
    targets = z_tiles + 2
    before, after = column[-1], column[1 % sizes[2]]

    def messages(sources, offsets, extra, waits, name):
        n_columns = sum(len(o) for o in offsets)
        extras = [] if extra is None else [extra]
        return call(
            functools.partial(radial_kernel, offsets, z_tiles, extra is not None),
            shape((targets, tile, width), jnp.float32),
            payload,
            before,
            after,
            *sources,
            radial_mix,
            *extras,
            scratch=[
                pltpu.VMEM((2, NRBF * tile, n_columns * tile), jnp.bfloat16),
                pltpu.VMEM((z_tiles, n_columns * tile, width), jnp.bfloat16),
            ],
            after=waits,
            name=name,
        )

    message = messages([middle], [ring[3:6]], None, [line], "radial_near")
    scale = 1.0 / math.sqrt(atoms * sizes[0] * sizes[1] * sizes[2])
    spot = place[2] * waves + place[0] * block
    mine_filters = lax.dynamic_slice_in_dim(filters, spot, block, axis=0)
    filtered = call(
        functools.partial(mix_kernel, scale),
        shape((2 * block, width), jnp.bfloat16),
        mine_filters,
        mix_weight,
        *lines,
        after=[message],
        name="mix",
    )
    blocks = [filtered] + [shift(filtered, "gx", -n) for n in range(1, n_blocks)]
    message = messages([west, east], [ring[:3], ring[6:]], message, [filtered], "radial_far")
    sums = call(
        functools.partial(long_kernel, z_tiles, n_blocks),
        [shape((atoms, width), jnp.float32)] * sizes[2],
        table,
        message,
        *blocks,
        name="longrange",
    )
    sums = [sums[0]] + [shift(sums[step], "gz", step) for step in range(1, sizes[2])]
    updated = call(
        node_kernel,
        shape((atoms, width), jnp.bfloat16),
        features.reshape(atoms, width),
        norm_gain.reshape(1, width),
        up_weight,
        down_weight,
        *sums,
        keep=False,
        name="node",
    )
    return updated.reshape(features.shape)


def fits(mesh, features, wavevectors):
    count_x, count_y, count_z, tile, width = features
    per = mesh.shape["gx"] * mesh.shape["gz"]
    lengths = [n * GRID for n in (count_x, count_y, count_z)]
    return (
        count_x == mesh.shape["gx"]
        and count_y == mesh.shape["gy"]
        and tile == 128
        and width == 128
        and wavevectors[1] % (16 * per) == 0
        and all(n & (n - 1) == 0 and n <= 2**14 for n in lengths)
    )


def solution(mesh):
    in_specs = (
        P("gx", "gy", "gz", None, None),
        P(None, "gx", "gy", "gz", None),
        P(),
        P(),
        P(),
        P(),
        P(),
        P(),
        P(),
        P(),
    )
    out_specs = P("gx", "gy", "gz", None, None)

    def layer(*args):
        body = fast_device if fits(mesh, args[0].shape, args[2].shape) else on_device
        return jax.shard_map(
            body, mesh=mesh, in_specs=in_specs, out_specs=out_specs, check_vma=False
        )(*args)

    return layer
```

```python
import functools
import math

import jax
import jax.numpy as jnp
import numpy as np
from jax import lax
from jax.experimental import pallas as pl
from jax.experimental.pallas import tpu as pltpu
from jax.sharding import PartitionSpec as P

NRBF = 6
GRID = 64


SHARP = 18.0
TWO_PI = 2.0 * math.pi
EPS = 1e-06
CONTRACT_FIRST = (((0,), (0,)), ((), ()))


def extended(array, sides, width):
    for axis, dim in sides:
        size, length = (lax.axis_size(axis), array.shape[dim])
        up = [(i, (i + 1) % size) for i in range(size)]
        down = [(j, i) for i, j in up]
        last = lax.slice_in_dim(array, length - width, length, axis=dim)
        first = lax.slice_in_dim(array, 0, width, axis=dim)
        before = lax.ppermute(last, axis, up)
        after = lax.ppermute(first, axis, down)
        array = jnp.concatenate([before, array, after], axis=dim)
    return array


def radial_basis(center, nearby_pos):
    tile_size = center.shape[1]
    offsets = (
        jnp.stack(
            [lax.broadcasted_iota(jnp.int32, (3, 3, 3, 1), component) for component in range(3)]
        )
        - 1
    )
    coords = (nearby_pos + offsets * GRID).reshape(3, 27 * tile_size)
    displace = coords[:, None, :] - center[:, :, None]
    square = jnp.sum(displace * displace, axis=0)
    scaled_dist = jnp.sqrt(square.astype(jnp.float32)) / GRID
    inside = (square > 0) & (square < GRID * GRID)
    envelope = jnp.where(inside, (1.0 - scaled_dist * scaled_dist) ** 2, 0.0)
    centres = (jnp.arange(NRBF, dtype=jnp.float32) + 0.5) / NRBF
    radial = (
        jnp.exp(-SHARP * (scaled_dist[:, None, :] - centres[None, :, None]) ** 2)
        * envelope[:, None, :]
    )
    return radial.astype(jnp.bfloat16)


def phase_tables(wavevectors, coords, lengths):
    fraction = jnp.zeros((wavevectors.shape[1], coords.shape[1]), jnp.float32)
    for component in range(3):
        product = jnp.mod(
            wavevectors[component][:, None] * coords[component][None, :], lengths[component]
        )
        fraction = fraction + product.astype(jnp.float32) / lengths[component]
    phase_angle = TWO_PI * fraction
    return (jnp.cos(phase_angle).astype(jnp.bfloat16), jnp.sin(phase_angle).astype(jnp.bfloat16))


def filter_mix(filters, factor, mix_weight):
    return jnp.dot(filters * factor, mix_weight, precision=lax.Precision.HIGHEST).astype(
        jnp.bfloat16
    )


def on_device(
    features,
    positions,
    wavevectors,
    radial_mix,
    charge_weight,
    filters,
    mix_weight,
    norm_gain,
    up_weight,
    down_weight,
):
    count_x, count_y, count_z, tile_size, feat_width = features.shape
    beside_all = extended(features, (("gx", 0), ("gy", 1), ("gz", 2)), 1)
    around_pos = extended(positions, (("gx", 1), ("gy", 2), ("gz", 3)), 1)
    anchor = jnp.zeros((), jnp.int32)

    def one_tile(flat_index):
        tile_x = flat_index // (count_y * count_z)
        tile_y = flat_index // count_z % count_y
        tile_z = flat_index % count_z
        neighbour = lax.dynamic_slice(
            beside_all, (tile_x, tile_y, tile_z, anchor, anchor), (3, 3, 3, tile_size, feat_width)
        )
        nearby_pos = lax.dynamic_slice(
            around_pos, (anchor, tile_x, tile_y, tile_z, anchor), (3, 3, 3, 3, tile_size)
        )
        center = lax.dynamic_slice(
            positions, (anchor, tile_x, tile_y, tile_z, anchor), (3, 1, 1, 1, tile_size)
        ).reshape(3, tile_size)
        radial = radial_basis(center, nearby_pos)
        pooled = jnp.einsum(
            "irj,jd->ird",
            radial,
            neighbour.reshape(27 * tile_size, feat_width),
            preferred_element_type=jnp.float32,
        )
        pooled = pooled.astype(jnp.bfloat16).reshape(tile_size, -1)
        return jnp.dot(pooled, radial_mix, preferred_element_type=jnp.float32)

    message = lax.map(one_tile, jnp.arange(count_x * count_y * count_z, dtype=jnp.int32))
    message = message.reshape(count_x * count_y * count_z * tile_size, feat_width)
    atom_count = count_x * count_y * count_z * tile_size
    counts = (count_x, count_y, count_z)
    axis_sizes = (lax.axis_size("gx"), lax.axis_size("gy"), lax.axis_size("gz"))
    axis_index = (lax.axis_index("gx"), lax.axis_index("gy"), lax.axis_index("gz"))
    lengths = tuple((counts[component] * axis_sizes[component] * GRID for component in range(3)))
    coords = jnp.stack(
        [
            (
                axis_index[component] * counts[component]
                + lax.broadcasted_iota(jnp.int32, (count_x, count_y, count_z, tile_size), component)
            )
            * GRID
            + positions[component]
            for component in range(3)
        ]
    ).reshape(3, atom_count)
    cos_table, sin_table = phase_tables(wavevectors, coords, lengths)
    charges = jnp.dot(
        features.reshape(atom_count, feat_width), charge_weight, preferred_element_type=jnp.float32
    ).astype(jnp.bfloat16)
    partial_cos = jnp.dot(cos_table, charges, preferred_element_type=jnp.float32)
    partial_sin = jnp.dot(sin_table, charges, preferred_element_type=jnp.float32)
    scale = 1.0 / math.sqrt(atom_count * axis_sizes[0] * axis_sizes[1] * axis_sizes[2])
    summed_cos, summed_sin = lax.psum((partial_cos, partial_sin), ("gx", "gy", "gz"))
    filtered_cos = filter_mix(filters, summed_cos * scale, mix_weight)
    filtered_sin = filter_mix(filters, summed_sin * scale, mix_weight)
    longrange = lax.dot_general(
        cos_table, filtered_cos, CONTRACT_FIRST, preferred_element_type=jnp.float32
    )
    longrange = longrange + lax.dot_general(
        sin_table, filtered_sin, CONTRACT_FIRST, preferred_element_type=jnp.float32
    )
    flat_sum = features.reshape(atom_count, feat_width).astype(jnp.float32) + message + longrange
    normed = (
        flat_sum
        * lax.rsqrt(jnp.mean(flat_sum * flat_sum, axis=-1, keepdims=True) + EPS)
        * norm_gain
    )
    hidden = jax.nn.silu(
        jnp.dot(normed.astype(jnp.bfloat16), up_weight, preferred_element_type=jnp.float32)
    ).astype(jnp.bfloat16)
    updated = flat_sum + jnp.dot(hidden, down_weight, preferred_element_type=jnp.float32)
    return updated.reshape(features.shape).astype(jnp.bfloat16)


LOG2E = 1.4426950408889634
POS_ROWS = 16
ROUND = 12582912.0
PIECE = 2
VMEM_GRANT = 16 * 2**20


def shift(array, axis, step):
    size = lax.axis_size(axis)
    return lax.ppermute(array, axis, [(i, (i + step) % size) for i in range(size)])


def sin_coefficients():
    nodes = np.cos((np.arange(400) + 0.5) / 400 * np.pi) * 0.25
    powers = np.stack([nodes ** (2 * n + 1) for n in range(5)], axis=1)
    scale = np.abs(powers).max(axis=0)
    fit = np.linalg.lstsq(powers / scale, np.sin(2 * np.pi * nodes), rcond=None)[0] / scale
    return [float(value) for value in fit]


SIN_FIT = sin_coefficients()


def sin_turns(u):
    square = u * u
    value = square * SIN_FIT[-1] + SIN_FIT[-2]
    for coefficient in SIN_FIT[-3::-1]:
        value = value * square + coefficient
    return value * u


def from_nearest(turns):
    return turns - ((turns + ROUND) - ROUND)


def table_kernel(n_blocks, z_tiles, place_ref, waves_ref, charge_ref, *refs):
    z_size = len(refs) - 2 - n_blocks
    columns, copy_ref, table_ref, parts = refs[:z_size], *refs[z_size : z_size + 2], refs[z_size + 2 :]
    copy_ref[...] = columns[0][...]
    tile = columns[0].shape[2]
    block = waves_ref.shape[1] // n_blocks
    row = lax.broadcasted_iota(jnp.int32, (POS_ROWS, tile), 0)
    coords, charges = [], []
    for step in range(z_size):
        for t in range(z_tiles):
            pos = columns[step][t, tile : tile + POS_ROWS, :].astype(jnp.float32)
            z = lax.rem(place_ref[2] + step, z_size) * z_tiles + t
            pos = jnp.where(row == 3, place_ref[0].astype(jnp.float32), pos)
            pos = jnp.where(row == 4, place_ref[1].astype(jnp.float32), pos)
            pos = jnp.where(row == 5, z.astype(jnp.float32), pos)
            coords.append(pos.astype(jnp.bfloat16))
            charges.append(
                jnp.dot(
                    columns[step][t, :tile, :], charge_ref[...], preferred_element_type=jnp.float32
                ).astype(jnp.bfloat16)
            )
    coords = jnp.concatenate(coords, axis=1)
    charges = jnp.concatenate(charges, axis=0)
    for n in range(n_blocks):
        turns = lax.dot_general(
            waves_ref[:, n * block : (n + 1) * block],
            coords,
            CONTRACT_FIRST,
            preferred_element_type=jnp.float32,
        )
        cos_part = sin_turns(0.25 - jnp.abs(from_nearest(turns)))
        sin_part = sin_turns(0.25 - jnp.abs(from_nearest(turns - 0.25)))
        base = 2 * n * block
        table_ref[base : base + block, :] = cos_part.astype(jnp.bfloat16)
        table_ref[base + block : base + 2 * block, :] = sin_part.astype(jnp.bfloat16)
        parts[n][...] = jnp.dot(
            table_ref[base : base + 2 * block, :], charges, preferred_element_type=jnp.float32
        ).astype(jnp.bfloat16)


def add_kernel(*refs):
    total = refs[0][...].astype(jnp.float32)
    for ref in refs[1:-1]:
        total = total + ref[...].astype(jnp.float32)
    refs[-1][...] = total.astype(refs[-1].dtype)


def mix_kernel(scale, filters_ref, mix_ref, *refs):
    total = refs[0][...].astype(jnp.float32)
    for ref in refs[1:-1]:
        total = total + ref[...].astype(jnp.float32)
    both = jnp.concatenate([filters_ref[...], filters_ref[...]], axis=0)
    refs[-1][...] = jnp.dot(
        both * (total * scale),
        mix_ref[...],
        precision=lax.Precision.HIGHEST,
        preferred_element_type=jnp.float32,
    ).astype(jnp.bfloat16)


def rows_of(row, values):
    out = jnp.zeros(row.shape, jnp.float32)
    for n, value in enumerate(values):
        out = jnp.where(row == n, value, out)
    return out.astype(jnp.bfloat16)


def split_norm(x, y, z):
    norm = x * x + y * y + z * z
    high = jnp.floor(norm * 16.0) * 0.0625
    return high, norm - high


def radial_kernel(offsets, z_tiles, has_extra, *refs):
    own_ref, before_ref, after_ref = refs[:3]
    groups = refs[3 : 3 + len(offsets)]
    mix_ref = refs[3 + len(offsets)]
    extra_ref = refs[4 + len(offsets)] if has_extra else None
    out_ref, radial_ref, feature_ref = refs[-3:]
    tile = own_ref.shape[2]
    row = lax.broadcasted_iota(jnp.int32, (POS_ROWS, tile), 0)
    columns = [(g, c, dx, dy) for g, per in enumerate(offsets) for c, (dx, dy) in enumerate(per)]

    def unit(ref_rows):
        pos = ref_rows.astype(jnp.float32) * (1.0 / GRID)
        return pos[0:1, :], pos[1:2, :], pos[2:3, :]

    sources = {}
    for slot, (g, c, dx, dy) in enumerate(columns):
        for sz in range(z_tiles):
            x, y, z = unit(groups[g][c, sz, tile : tile + POS_ROWS, :])
            high, low = split_norm(x, y, z)
            one = jnp.ones_like(x)
            sources[slot, sz] = rows_of(row, [x, y, z, one, one, high, low])
            feature_ref[sz, slot * tile : (slot + 1) * tile, :] = groups[g][c, sz, :tile, :]
    targets = [(-1, before_ref, z_tiles - 1)]
    targets += [(t, own_ref, t) for t in range(z_tiles)]
    targets += [(z_tiles, after_ref, 0)]
    blocks = [
        (index, sz)
        for index, (tz, ref, at) in enumerate(targets)
        for sz in range(z_tiles)
        if abs(sz - tz) <= 1
    ]
    pooled = {}

    def basis(block_at, slot):
        index, sz = blocks[block_at]
        tz, ref, at = targets[index]
        dx, dy = columns[slot][2:]
        x0, y0, z0 = unit(ref[at, tile : tile + POS_ROWS, :])
        x, y, z = x0 - dx, y0 - dy, z0 - (sz - tz)
        high, low = split_norm(x, y, z)
        one = jnp.ones_like(x)
        target = rows_of(row, [-2 * x, -2 * y, -2 * z, high, low, one, one])
        square = lax.dot_general(
            target, sources[slot, sz], CONTRACT_FIRST, preferred_element_type=jnp.float32
        )
        square = jnp.where(square == 0.0, 1.0, jnp.minimum(square, 1.0))
        dist = square * lax.rsqrt(square)
        lack = 1.0 - square
        value = jnp.exp2(dist * (3.0 * LOG2E - (SHARP * LOG2E) * dist)) * (lack * lack)
        growth = jnp.exp2(dist * (6.0 * LOG2E))
        for r in range(NRBF):
            radial_ref[
                block_at % 2, r * tile : (r + 1) * tile, slot * tile : (slot + 1) * tile
            ] = value.astype(jnp.bfloat16)
            if r + 1 < NRBF:
                value = value * growth

    def pool(block_at, r):
        index, sz = blocks[block_at]
        part = jnp.dot(
            radial_ref[block_at % 2, r * tile : (r + PIECE) * tile, :],
            feature_ref[sz],
            preferred_element_type=jnp.float32,
        )
        for step in range(PIECE):
            piece = part[step * tile : (step + 1) * tile, :]
            key = index, r + step
            pooled[key] = pooled[key] + piece if key in pooled else piece

    def finish(index):
        message = extra_ref[index] if has_extra else None
        for r in range(NRBF):
            level = math.exp(-SHARP * ((r + 0.5) / NRBF) ** 2)
            part = jnp.dot(
                (pooled.pop((index, r)) * level).astype(jnp.bfloat16),
                mix_ref[r * tile : (r + 1) * tile, :],
                preferred_element_type=jnp.float32,
            )
            message = part if message is None else message + part
        out_ref[index] = message

    n_pieces = NRBF // PIECE
    for block_at in range(len(blocks) + 1):
        work = []
        if block_at < len(blocks):
            work += [(slot / len(columns), 0, slot) for slot in range(len(columns))]
        if block_at > 0:
            work += [((n + 0.5) / n_pieces, 1, n) for n in range(n_pieces)]
        for _, kind, n in sorted(work):
            if kind:
                pool(block_at - 1, n * PIECE)
            else:
                basis(block_at, n)
        if block_at > 0:
            index = blocks[block_at - 1][0]
            if block_at == len(blocks) or blocks[block_at][0] != index:
                finish(index)


def long_kernel(z_tiles, n_blocks, table_ref, message_ref, *refs):
    blocks, outs = refs[:n_blocks], refs[n_blocks:]
    z_size, tile = len(outs), message_ref.shape[1]
    filtered = jnp.concatenate([ref[...] for ref in blocks], axis=0)
    flipped = lax.dot_general(
        filtered, table_ref[...], CONTRACT_FIRST, preferred_element_type=jnp.float32
    )
    for step in range(z_size):
        for t in range(z_tiles):
            at = (step * z_tiles + t) * tile
            value = flipped[:, at : at + tile].T
            if step == 0:
                value = value + message_ref[1 + t]
            if step == (z_size - 1) % z_size and t == z_tiles - 1:
                value = value + message_ref[0]
            if step == 1 % z_size and t == 0:
                value = value + message_ref[z_tiles + 1]
            outs[step][t * tile : (t + 1) * tile, :] = value


def node_kernel(features_ref, gain_ref, up_ref, down_ref, *refs):
    total = features_ref[...].astype(jnp.float32)
    for ref in refs[:-1]:
        total = total + ref[...]
    normed = (
        total
        * lax.rsqrt(jnp.mean(total * total, axis=-1, keepdims=True) + EPS)
        * gain_ref[...]
    )
    inner = jnp.dot(normed.astype(jnp.bfloat16), up_ref[...], preferred_element_type=jnp.float32)
    hidden = (inner / (1.0 + jnp.exp(-inner))).astype(jnp.bfloat16)
    updated = total + jnp.dot(hidden, down_ref[...], preferred_element_type=jnp.float32)
    refs[-1][...] = updated.astype(jnp.bfloat16)


def call(kernel, out_shape, *args, scalars=0, after=(), scratch=(), keep=True):
    in_vmem = pl.BlockSpec(memory_space=pltpu.VMEM)
    anywhere = pl.BlockSpec(memory_space=pl.ANY)
    single = not isinstance(out_shape, (list, tuple))
    held = [pltpu.with_memory_space_constraint(a, pltpu.VMEM) for a in args[scalars:]]
    n_args, n_after = len(args), len(after)
    if keep:
        out_shape = jax.tree.map(lambda o: pltpu.VMEM(o.shape, o.dtype), out_shape)

    def body(*refs):
        kernel(*refs[:n_args], *refs[n_args + n_after :])

    return pl.pallas_call(
        body,
        out_shape=out_shape,
        in_specs=[pl.BlockSpec(memory_space=pltpu.SMEM)] * scalars
        + [in_vmem] * len(held)
        + [anywhere] * n_after,
        out_specs=in_vmem if single else [in_vmem] * len(out_shape),
        scratch_shapes=list(scratch),
        compiler_params=pltpu.CompilerParams(vmem_limit_bytes=VMEM_GRANT),
    )(*args[:scalars], *held, *after)


def fast_device(
    features,
    positions,
    wavevectors,
    radial_mix,
    charge_weight,
    filters,
    mix_weight,
    norm_gain,
    up_weight,
    down_weight,
):
    z_tiles, tile, width = features.shape[2:]
    sizes = tuple(lax.axis_size(axis) for axis in ("gx", "gy", "gz"))
    place = jnp.stack([lax.axis_index(axis) for axis in ("gx", "gy", "gz")]).astype(jnp.int32)
    counts = (sizes[0], sizes[1], sizes[2] * z_tiles)
    n_blocks, waves = sizes[0], wavevectors.shape[1] // sizes[2]
    block = waves // n_blocks
    atoms = z_tiles * tile
    shape = jax.ShapeDtypeStruct

    pos = jnp.moveaxis(positions.reshape(3, z_tiles, tile), 0, 1).astype(jnp.bfloat16)
    payload = jnp.concatenate(
        [
            features.reshape(z_tiles, tile, width),
            jnp.pad(pos, ((0, 0), (0, POS_ROWS - 3), (0, 0))),
        ],
        axis=1,
    )
    column = [payload] + [shift(payload, "gz", -step) for step in range(1, sizes[2])]
    mine = lax.dynamic_slice_in_dim(wavevectors, place[2] * waves, waves, axis=1)
    mine = jnp.concatenate([mine, mine], axis=1)
    mine = lax.dynamic_slice_in_dim(mine, place[0] * block, waves, axis=1).astype(jnp.float32)
    fine = jnp.array([1.0 / (count * GRID) for count in counts], jnp.float32)[:, None]
    coarse = jnp.array([1.0 / count for count in counts], jnp.float32)[:, None]
    mine = jnp.concatenate([mine * fine, mine * coarse], axis=0)
    mine = jnp.pad(mine, ((0, POS_ROWS - 6), (0, 0))).astype(jnp.bfloat16)

    later, table, *parts = call(
        functools.partial(table_kernel, n_blocks, z_tiles),
        [shape(payload.shape, payload.dtype), shape((2 * waves, sizes[2] * atoms), jnp.bfloat16)]
        + [shape((2 * block, width), jnp.bfloat16)] * n_blocks,
        place,
        mine,
        charge_weight,
        *column,
        scalars=1,
    )
    south, north = shift(later, "gy", 1), shift(later, "gy", -1)
    middle = jnp.stack([south, later, north])
    arrived = [parts[0]] + [shift(parts[n], "gx", n) for n in range(1, n_blocks)]
    west, east = shift(middle, "gx", 1), shift(middle, "gx", -1)
    line = call(add_kernel, shape((2 * block, width), jnp.bfloat16), *arrived)
    lines = [line] + [shift(line, "gy", n) for n in range(1, sizes[1])]

    ring = [(dx, dy) for dx in (-1, 0, 1) for dy in (-1, 0, 1)]
    targets = z_tiles + 2
    before, after = column[-1], column[1 % sizes[2]]

    def messages(sources, offsets, extra, waits):
        n_columns = sum(len(o) for o in offsets)
        extras = [] if extra is None else [extra]
        return call(
            functools.partial(radial_kernel, offsets, z_tiles, extra is not None),
            shape((targets, tile, width), jnp.float32),
            payload,
            before,
            after,
            *sources,
            radial_mix,
            *extras,
            scratch=[
                pltpu.VMEM((2, NRBF * tile, n_columns * tile), jnp.bfloat16),
                pltpu.VMEM((z_tiles, n_columns * tile, width), jnp.bfloat16),
            ],
            after=waits,
        )

    message = messages([middle], [ring[3:6]], None, [line])
    scale = 1.0 / math.sqrt(atoms * sizes[0] * sizes[1] * sizes[2])
    spot = place[2] * waves + place[0] * block
    mine_filters = lax.dynamic_slice_in_dim(filters, spot, block, axis=0)
    filtered = call(
        functools.partial(mix_kernel, scale),
        shape((2 * block, width), jnp.bfloat16),
        mine_filters,
        mix_weight,
        *lines,
        after=[message],
    )
    blocks = [filtered] + [shift(filtered, "gx", -n) for n in range(1, n_blocks)]
    message = messages([west], [ring[:3]], message, [filtered])
    message = messages([east], [ring[6:]], message, [])
    sums = call(
        functools.partial(long_kernel, z_tiles, n_blocks),
        [shape((atoms, width), jnp.float32)] * sizes[2],
        table,
        message,
        *blocks,
    )
    sums = [sums[0]] + [shift(sums[step], "gz", step) for step in range(1, sizes[2])]
    updated = call(
        node_kernel,
        shape((atoms, width), jnp.bfloat16),
        features.reshape(atoms, width),
        norm_gain.reshape(1, width),
        up_weight,
        down_weight,
        *sums,
        keep=False,
    )
    return updated.reshape(features.shape)


def fits(mesh, features, wavevectors):
    count_x, count_y, count_z, tile, width = features
    per = mesh.shape["gx"] * mesh.shape["gz"]
    lengths = [n * GRID for n in (count_x, count_y, count_z)]
    return (
        count_x == mesh.shape["gx"]
        and count_y == mesh.shape["gy"]
        and tile == 128
        and width == 128
        and wavevectors[1] % (16 * per) == 0
        and all(n & (n - 1) == 0 and n <= 2**14 for n in lengths)
    )


def solution(mesh):
    in_specs = (
        P("gx", "gy", "gz", None, None),
        P(None, "gx", "gy", "gz", None),
        P(),
        P(),
        P(),
        P(),
        P(),
        P(),
        P(),
        P(),
    )
    out_specs = P("gx", "gy", "gz", None, None)

    def fast(*args):
        return fast_device(*args)

    def layer(*args):
        quick = fits(mesh, args[0].shape, args[2].shape)
        mapped = jax.shard_map(
            fast if quick else on_device,
            mesh=mesh,
            in_specs=in_specs,
            out_specs=out_specs,
            check_vma=False,
        )
        return mapped(*args)

    return layer
```

```python
import functools
import math

import jax
import jax.numpy as jnp
import numpy as np
from jax import lax
from jax.experimental import pallas as pl
from jax.experimental.pallas import tpu as pltpu
from jax.sharding import PartitionSpec as P

NRBF = 6
GRID = 64


SHARP = 18.0
TWO_PI = 2.0 * math.pi
EPS = 1e-06
CONTRACT_FIRST = (((0,), (0,)), ((), ()))


def extended(array, sides, width):
    for axis, dim in sides:
        size, length = (lax.axis_size(axis), array.shape[dim])
        up = [(i, (i + 1) % size) for i in range(size)]
        down = [(j, i) for i, j in up]
        last = lax.slice_in_dim(array, length - width, length, axis=dim)
        first = lax.slice_in_dim(array, 0, width, axis=dim)
        before = lax.ppermute(last, axis, up)
        after = lax.ppermute(first, axis, down)
        array = jnp.concatenate([before, array, after], axis=dim)
    return array


def radial_basis(center, nearby_pos):
    tile_size = center.shape[1]
    offsets = (
        jnp.stack(
            [lax.broadcasted_iota(jnp.int32, (3, 3, 3, 1), component) for component in range(3)]
        )
        - 1
    )
    coords = (nearby_pos + offsets * GRID).reshape(3, 27 * tile_size)
    displace = coords[:, None, :] - center[:, :, None]
    square = jnp.sum(displace * displace, axis=0)
    scaled_dist = jnp.sqrt(square.astype(jnp.float32)) / GRID
    inside = (square > 0) & (square < GRID * GRID)
    envelope = jnp.where(inside, (1.0 - scaled_dist * scaled_dist) ** 2, 0.0)
    centres = (jnp.arange(NRBF, dtype=jnp.float32) + 0.5) / NRBF
    radial = (
        jnp.exp(-SHARP * (scaled_dist[:, None, :] - centres[None, :, None]) ** 2)
        * envelope[:, None, :]
    )
    return radial.astype(jnp.bfloat16)


def phase_tables(wavevectors, coords, lengths):
    fraction = jnp.zeros((wavevectors.shape[1], coords.shape[1]), jnp.float32)
    for component in range(3):
        product = jnp.mod(
            wavevectors[component][:, None] * coords[component][None, :], lengths[component]
        )
        fraction = fraction + product.astype(jnp.float32) / lengths[component]
    phase_angle = TWO_PI * fraction
    return (jnp.cos(phase_angle).astype(jnp.bfloat16), jnp.sin(phase_angle).astype(jnp.bfloat16))


def filter_mix(filters, factor, mix_weight):
    return jnp.dot(filters * factor, mix_weight, precision=lax.Precision.HIGHEST).astype(
        jnp.bfloat16
    )


def on_device(
    features,
    positions,
    wavevectors,
    radial_mix,
    charge_weight,
    filters,
    mix_weight,
    norm_gain,
    up_weight,
    down_weight,
):
    count_x, count_y, count_z, tile_size, feat_width = features.shape
    beside_all = extended(features, (("gx", 0), ("gy", 1), ("gz", 2)), 1)
    around_pos = extended(positions, (("gx", 1), ("gy", 2), ("gz", 3)), 1)
    anchor = jnp.zeros((), jnp.int32)

    def one_tile(flat_index):
        tile_x = flat_index // (count_y * count_z)
        tile_y = flat_index // count_z % count_y
        tile_z = flat_index % count_z
        neighbour = lax.dynamic_slice(
            beside_all, (tile_x, tile_y, tile_z, anchor, anchor), (3, 3, 3, tile_size, feat_width)
        )
        nearby_pos = lax.dynamic_slice(
            around_pos, (anchor, tile_x, tile_y, tile_z, anchor), (3, 3, 3, 3, tile_size)
        )
        center = lax.dynamic_slice(
            positions, (anchor, tile_x, tile_y, tile_z, anchor), (3, 1, 1, 1, tile_size)
        ).reshape(3, tile_size)
        radial = radial_basis(center, nearby_pos)
        pooled = jnp.einsum(
            "irj,jd->ird",
            radial,
            neighbour.reshape(27 * tile_size, feat_width),
            preferred_element_type=jnp.float32,
        )
        pooled = pooled.astype(jnp.bfloat16).reshape(tile_size, -1)
        return jnp.dot(pooled, radial_mix, preferred_element_type=jnp.float32)

    message = lax.map(one_tile, jnp.arange(count_x * count_y * count_z, dtype=jnp.int32))
    message = message.reshape(count_x * count_y * count_z * tile_size, feat_width)
    atom_count = count_x * count_y * count_z * tile_size
    counts = (count_x, count_y, count_z)
    axis_sizes = (lax.axis_size("gx"), lax.axis_size("gy"), lax.axis_size("gz"))
    axis_index = (lax.axis_index("gx"), lax.axis_index("gy"), lax.axis_index("gz"))
    lengths = tuple((counts[component] * axis_sizes[component] * GRID for component in range(3)))
    coords = jnp.stack(
        [
            (
                axis_index[component] * counts[component]
                + lax.broadcasted_iota(jnp.int32, (count_x, count_y, count_z, tile_size), component)
            )
            * GRID
            + positions[component]
            for component in range(3)
        ]
    ).reshape(3, atom_count)
    cos_table, sin_table = phase_tables(wavevectors, coords, lengths)
    charges = jnp.dot(
        features.reshape(atom_count, feat_width), charge_weight, preferred_element_type=jnp.float32
    ).astype(jnp.bfloat16)
    partial_cos = jnp.dot(cos_table, charges, preferred_element_type=jnp.float32)
    partial_sin = jnp.dot(sin_table, charges, preferred_element_type=jnp.float32)
    scale = 1.0 / math.sqrt(atom_count * axis_sizes[0] * axis_sizes[1] * axis_sizes[2])
    summed_cos, summed_sin = lax.psum((partial_cos, partial_sin), ("gx", "gy", "gz"))
    filtered_cos = filter_mix(filters, summed_cos * scale, mix_weight)
    filtered_sin = filter_mix(filters, summed_sin * scale, mix_weight)
    longrange = lax.dot_general(
        cos_table, filtered_cos, CONTRACT_FIRST, preferred_element_type=jnp.float32
    )
    longrange = longrange + lax.dot_general(
        sin_table, filtered_sin, CONTRACT_FIRST, preferred_element_type=jnp.float32
    )
    flat_sum = features.reshape(atom_count, feat_width).astype(jnp.float32) + message + longrange
    normed = (
        flat_sum
        * lax.rsqrt(jnp.mean(flat_sum * flat_sum, axis=-1, keepdims=True) + EPS)
        * norm_gain
    )
    hidden = jax.nn.silu(
        jnp.dot(normed.astype(jnp.bfloat16), up_weight, preferred_element_type=jnp.float32)
    ).astype(jnp.bfloat16)
    updated = flat_sum + jnp.dot(hidden, down_weight, preferred_element_type=jnp.float32)
    return updated.reshape(features.shape).astype(jnp.bfloat16)


LOG2E = 1.4426950408889634
POS_ROWS = 16
ROUND = 12582912.0
PIECE = 2
VMEM_GRANT = 16 * 2**20


def shift(array, axis, step):
    size = lax.axis_size(axis)
    return lax.ppermute(array, axis, [(i, (i + step) % size) for i in range(size)])


def sin_coefficients():
    nodes = np.cos((np.arange(400) + 0.5) / 400 * np.pi) * 0.25
    powers = np.stack([nodes ** (2 * n + 1) for n in range(5)], axis=1)
    scale = np.abs(powers).max(axis=0)
    fit = np.linalg.lstsq(powers / scale, np.sin(2 * np.pi * nodes), rcond=None)[0] / scale
    return [float(value) for value in fit]


SIN_FIT = sin_coefficients()


def sin_turns(u):
    square = u * u
    value = square * SIN_FIT[-1] + SIN_FIT[-2]
    for coefficient in SIN_FIT[-3::-1]:
        value = value * square + coefficient
    return value * u


def from_nearest(turns):
    return turns - ((turns + ROUND) - ROUND)


def payload_kernel(features_ref, positions_ref, out_ref, held_ref, sems):
    z_tiles, tile, width = features_ref.shape
    move = pltpu.make_async_copy(features_ref, out_ref.at[:, pl.ds(0, tile), :], sems.at[0])
    fetch = pltpu.make_async_copy(positions_ref, held_ref, sems.at[1])
    fetch.start()
    move.start()
    fetch.wait()
    row = lax.broadcasted_iota(jnp.int32, (POS_ROWS, width), 0)
    for t in range(z_tiles):
        rows = jnp.zeros((POS_ROWS, width), jnp.float32)
        for c in range(3):
            pos = held_ref[c, t : t + 1, :].astype(jnp.float32)
            rows = jnp.where(row == c, pos, rows)
        out_ref[t, tile:, :] = rows.astype(jnp.bfloat16)
    move.wait()


def table_kernel(n_blocks, z_tiles, place_ref, waves_ref, charge_ref, gain_ref, *refs):
    z_size = len(refs) - 3 - n_blocks
    refs[-1][...] = gain_ref[...]
    columns, copy_ref, table_ref, parts = refs[:z_size], *refs[z_size : z_size + 2], refs[z_size + 2 : -1]
    copy_ref[...] = columns[0][...]
    tile = columns[0].shape[2]
    block = waves_ref.shape[1] // n_blocks
    row = lax.broadcasted_iota(jnp.int32, (POS_ROWS, tile), 0)
    coords, charges = [], []
    for step in range(z_size):
        for t in range(z_tiles):
            pos = columns[step][t, tile : tile + POS_ROWS, :].astype(jnp.float32)
            z = lax.rem(place_ref[2] + step, z_size) * z_tiles + t
            pos = jnp.where(row == 3, place_ref[0].astype(jnp.float32), pos)
            pos = jnp.where(row == 4, place_ref[1].astype(jnp.float32), pos)
            pos = jnp.where(row == 5, z.astype(jnp.float32), pos)
            coords.append(pos.astype(jnp.bfloat16))
            charges.append(
                jnp.dot(
                    columns[step][t, :tile, :], charge_ref[...], preferred_element_type=jnp.float32
                ).astype(jnp.bfloat16)
            )
    coords = jnp.concatenate(coords, axis=1)
    charges = jnp.concatenate(charges, axis=0)
    for n in range(n_blocks):
        turns = lax.dot_general(
            waves_ref[:, n * block : (n + 1) * block],
            coords,
            CONTRACT_FIRST,
            preferred_element_type=jnp.float32,
        )
        cos_part = sin_turns(0.25 - jnp.abs(from_nearest(turns)))
        sin_part = sin_turns(0.25 - jnp.abs(from_nearest(turns - 0.25)))
        base = 2 * n * block
        table_ref[base : base + block, :] = cos_part.astype(jnp.bfloat16)
        table_ref[base + block : base + 2 * block, :] = sin_part.astype(jnp.bfloat16)
        parts[n][...] = jnp.dot(
            table_ref[base : base + 2 * block, :], charges, preferred_element_type=jnp.float32
        ).astype(jnp.bfloat16)


def add_kernel(*refs):
    total = refs[0][...].astype(jnp.float32)
    for ref in refs[1:-1]:
        total = total + ref[...].astype(jnp.float32)
    refs[-1][...] = total.astype(refs[-1].dtype)


def mix_kernel(scale, filters_ref, mix_ref, *refs):
    total = refs[0][...].astype(jnp.float32)
    for ref in refs[1:-1]:
        total = total + ref[...].astype(jnp.float32)
    both = jnp.concatenate([filters_ref[...], filters_ref[...]], axis=0)
    refs[-1][...] = jnp.dot(
        both * (total * scale),
        mix_ref[...],
        precision=lax.Precision.HIGHEST,
        preferred_element_type=jnp.float32,
    ).astype(jnp.bfloat16)


def rows_of(row, values):
    out = jnp.zeros(row.shape, jnp.float32)
    for n, value in enumerate(values):
        out = jnp.where(row == n, value, out)
    return out.astype(jnp.bfloat16)


def split_norm(x, y, z):
    norm = x * x + y * y + z * z
    high = jnp.floor(norm * 16.0) * 0.0625
    return high, norm - high


def radial_kernel(offsets, z_tiles, has_extra, *refs):
    own_ref, before_ref, after_ref = refs[:3]
    groups = refs[3 : 3 + len(offsets)]
    mix_ref = refs[3 + len(offsets)]
    extra_ref = refs[4 + len(offsets)] if has_extra else None
    out_ref, radial_ref, feature_ref = refs[-3:]
    tile = own_ref.shape[2]
    row = lax.broadcasted_iota(jnp.int32, (POS_ROWS, tile), 0)
    columns = [(g, c, dx, dy) for g, per in enumerate(offsets) for c, (dx, dy) in enumerate(per)]

    def unit(ref_rows):
        pos = ref_rows.astype(jnp.float32) * (1.0 / GRID)
        return pos[0:1, :], pos[1:2, :], pos[2:3, :]

    sources = {}
    for slot, (g, c, dx, dy) in enumerate(columns):
        for sz in range(z_tiles):
            x, y, z = unit(groups[g][c, sz, tile : tile + POS_ROWS, :])
            high, low = split_norm(x, y, z)
            one = jnp.ones_like(x)
            sources[slot, sz] = rows_of(row, [x, y, z, one, one, high, low])
            feature_ref[sz, slot * tile : (slot + 1) * tile, :] = groups[g][c, sz, :tile, :]
    targets = [(-1, before_ref, z_tiles - 1)]
    targets += [(t, own_ref, t) for t in range(z_tiles)]
    targets += [(z_tiles, after_ref, 0)]
    blocks = [
        (index, sz)
        for index, (tz, ref, at) in enumerate(targets)
        for sz in range(z_tiles)
        if abs(sz - tz) <= 1
    ]
    pooled = {}

    def basis(block_at, slot):
        index, sz = blocks[block_at]
        tz, ref, at = targets[index]
        dx, dy = columns[slot][2:]
        x0, y0, z0 = unit(ref[at, tile : tile + POS_ROWS, :])
        x, y, z = x0 - dx, y0 - dy, z0 - (sz - tz)
        high, low = split_norm(x, y, z)
        one = jnp.ones_like(x)
        target = rows_of(row, [-2 * x, -2 * y, -2 * z, high, low, one, one])
        square = lax.dot_general(
            target, sources[slot, sz], CONTRACT_FIRST, preferred_element_type=jnp.float32
        )
        square = jnp.where(square == 0.0, 1.0, jnp.minimum(square, 1.0))
        dist = square * lax.rsqrt(square)
        lack = 1.0 - square
        value = jnp.exp2(dist * (3.0 * LOG2E - (SHARP * LOG2E) * dist)) * (lack * lack)
        growth = jnp.exp2(dist * (6.0 * LOG2E))
        for r in range(NRBF):
            radial_ref[
                block_at % 2, r * tile : (r + 1) * tile, slot * tile : (slot + 1) * tile
            ] = value.astype(jnp.bfloat16)
            if r + 1 < NRBF:
                value = value * growth

    def pool(block_at, r):
        index, sz = blocks[block_at]
        part = jnp.dot(
            radial_ref[block_at % 2, r * tile : (r + PIECE) * tile, :],
            feature_ref[sz],
            preferred_element_type=jnp.float32,
        )
        for step in range(PIECE):
            piece = part[step * tile : (step + 1) * tile, :]
            key = index, r + step
            pooled[key] = pooled[key] + piece if key in pooled else piece

    def finish(index):
        message = extra_ref[index] if has_extra else None
        for r in range(NRBF):
            level = math.exp(-SHARP * ((r + 0.5) / NRBF) ** 2)
            part = jnp.dot(
                (pooled.pop((index, r)) * level).astype(jnp.bfloat16),
                mix_ref[r * tile : (r + 1) * tile, :],
                preferred_element_type=jnp.float32,
            )
            message = part if message is None else message + part
        out_ref[index] = message

    n_pieces = NRBF // PIECE
    for block_at in range(len(blocks) + 1):
        work = []
        if block_at < len(blocks):
            work += [(slot / len(columns), 0, slot) for slot in range(len(columns))]
        if block_at > 0:
            work += [((n + 0.5) / n_pieces, 1, n) for n in range(n_pieces)]
        for _, kind, n in sorted(work):
            if kind:
                pool(block_at - 1, n * PIECE)
            else:
                basis(block_at, n)
        if block_at > 0:
            index = blocks[block_at - 1][0]
            if block_at == len(blocks) or blocks[block_at][0] != index:
                finish(index)


def long_kernel(z_tiles, n_blocks, table_ref, message_ref, *refs):
    blocks, outs = refs[:n_blocks], refs[n_blocks:]
    z_size, tile = len(outs), message_ref.shape[1]
    filtered = jnp.concatenate([ref[...] for ref in blocks], axis=0)
    flipped = lax.dot_general(
        filtered, table_ref[...], CONTRACT_FIRST, preferred_element_type=jnp.float32
    )
    for step in range(z_size):
        for t in range(z_tiles):
            at = (step * z_tiles + t) * tile
            value = flipped[:, at : at + tile].T
            if step == 0:
                value = value + message_ref[1 + t]
            if step == (z_size - 1) % z_size and t == z_tiles - 1:
                value = value + message_ref[0]
            if step == 1 % z_size and t == 0:
                value = value + message_ref[z_tiles + 1]
            outs[step][t * tile : (t + 1) * tile, :] = value


def node_kernel(features_ref, gain_ref, up_ref, down_ref, *refs):
    total = features_ref[...].astype(jnp.float32)
    for ref in refs[:-1]:
        total = total + ref[...]
    normed = (
        total
        * lax.rsqrt(jnp.mean(total * total, axis=-1, keepdims=True) + EPS)
        * gain_ref[...]
    )
    inner = jnp.dot(normed.astype(jnp.bfloat16), up_ref[...], preferred_element_type=jnp.float32)
    hidden = (inner / (1.0 + jnp.exp(-inner))).astype(jnp.bfloat16)
    updated = total + jnp.dot(hidden, down_ref[...], preferred_element_type=jnp.float32)
    refs[-1][...] = updated.astype(jnp.bfloat16)


def call(kernel, out_shape, *args, scalars=0, after=(), scratch=(), keep=True, hold=True):
    in_vmem = pl.BlockSpec(memory_space=pltpu.VMEM)
    anywhere = pl.BlockSpec(memory_space=pl.ANY)
    single = not isinstance(out_shape, (list, tuple))
    space = pltpu.VMEM if hold else pltpu.HBM
    held = [pltpu.with_memory_space_constraint(a, space) for a in args[scalars:]]
    n_args, n_after = len(args), len(after)
    if keep:
        out_shape = jax.tree.map(lambda o: pltpu.VMEM(o.shape, o.dtype), out_shape)

    def body(*refs):
        kernel(*refs[:n_args], *refs[n_args + n_after :])

    return pl.pallas_call(
        body,
        out_shape=out_shape,
        in_specs=[pl.BlockSpec(memory_space=pltpu.SMEM)] * scalars
        + [in_vmem if hold else pl.BlockSpec(memory_space=pltpu.HBM)] * len(held)
        + [anywhere] * n_after,
        out_specs=in_vmem if single else [in_vmem] * len(out_shape),
        scratch_shapes=list(scratch),
        compiler_params=pltpu.CompilerParams(vmem_limit_bytes=VMEM_GRANT),
    )(*args[:scalars], *held, *after)


def fast_device(
    features,
    positions,
    wavevectors,
    radial_mix,
    charge_weight,
    filters,
    mix_weight,
    norm_gain,
    up_weight,
    down_weight,
):
    z_tiles, tile, width = features.shape[2:]
    sizes = tuple(lax.axis_size(axis) for axis in ("gx", "gy", "gz"))
    place = jnp.stack([lax.axis_index(axis) for axis in ("gx", "gy", "gz")]).astype(jnp.int32)
    counts = (sizes[0], sizes[1], sizes[2] * z_tiles)
    n_blocks, waves = sizes[0], wavevectors.shape[1] // sizes[2]
    block = waves // n_blocks
    atoms = z_tiles * tile
    shape = jax.ShapeDtypeStruct

    payload = call(
        payload_kernel,
        shape((z_tiles, tile + POS_ROWS, width), jnp.bfloat16),
        features.reshape(z_tiles, tile, width),
        positions.reshape(3, z_tiles, tile),
        hold=False,
        scratch=[pltpu.VMEM((3, z_tiles, tile), jnp.int32), pltpu.SemaphoreType.DMA((2,))],
    )
    column = [payload] + [shift(payload, "gz", -step) for step in range(1, sizes[2])]
    mine = lax.dynamic_slice_in_dim(wavevectors, place[2] * waves, waves, axis=1)
    mine = jnp.concatenate([mine, mine], axis=1)
    mine = lax.dynamic_slice_in_dim(mine, place[0] * block, waves, axis=1).astype(jnp.float32)
    fine = jnp.array([1.0 / (count * GRID) for count in counts], jnp.float32)[:, None]
    coarse = jnp.array([1.0 / count for count in counts], jnp.float32)[:, None]
    mine = jnp.concatenate([mine * fine, mine * coarse], axis=0)
    mine = jnp.pad(mine, ((0, POS_ROWS - 6), (0, 0))).astype(jnp.bfloat16)

    later, table, *parts, gain = call(
        functools.partial(table_kernel, n_blocks, z_tiles),
        [shape(payload.shape, payload.dtype), shape((2 * waves, sizes[2] * atoms), jnp.bfloat16)]
        + [shape((2 * block, width), jnp.bfloat16)] * n_blocks
        + [shape((1, width), jnp.float32)],
        place,
        mine,
        charge_weight,
        norm_gain.reshape(1, width),
        *column,
        scalars=1,
    )
    south, north = shift(later, "gy", 1), shift(later, "gy", -1)
    middle = jnp.stack([south, later, north])
    arrived = [parts[0]] + [shift(parts[n], "gx", n) for n in range(1, n_blocks)]
    west, east = shift(middle, "gx", 1), shift(middle, "gx", -1)
    line = call(add_kernel, shape((2 * block, width), jnp.bfloat16), *arrived)
    lines = [line] + [shift(line, "gy", n) for n in range(1, sizes[1])]

    ring = [(dx, dy) for dx in (-1, 0, 1) for dy in (-1, 0, 1)]
    targets = z_tiles + 2
    before, after = column[-1], column[1 % sizes[2]]

    def messages(sources, offsets, extra, waits):
        n_columns = sum(len(o) for o in offsets)
        extras = [] if extra is None else [extra]
        return call(
            functools.partial(radial_kernel, offsets, z_tiles, extra is not None),
            shape((targets, tile, width), jnp.float32),
            payload,
            before,
            after,
            *sources,
            radial_mix,
            *extras,
            scratch=[
                pltpu.VMEM((2, NRBF * tile, n_columns * tile), jnp.bfloat16),
                pltpu.VMEM((z_tiles, n_columns * tile, width), jnp.bfloat16),
            ],
            after=waits,
        )

    message = messages([middle], [ring[3:6]], None, [line])
    scale = 1.0 / math.sqrt(atoms * sizes[0] * sizes[1] * sizes[2])
    spot = place[2] * waves + place[0] * block
    mine_filters = lax.dynamic_slice_in_dim(filters, spot, block, axis=0)
    filtered = call(
        functools.partial(mix_kernel, scale),
        shape((2 * block, width), jnp.bfloat16),
        mine_filters,
        mix_weight,
        *lines,
        after=[message],
    )
    blocks = [filtered] + [shift(filtered, "gx", -n) for n in range(1, n_blocks)]
    message = messages([west], [ring[:3]], message, [filtered])
    message = messages([east], [ring[6:]], message, [])
    sums = call(
        functools.partial(long_kernel, z_tiles, n_blocks),
        [shape((atoms, width), jnp.float32)] * sizes[2],
        table,
        message,
        *blocks,
    )
    sums = [sums[0]] + [shift(sums[step], "gz", step) for step in range(1, sizes[2])]
    updated = call(
        node_kernel,
        shape((atoms, width), jnp.bfloat16),
        features.reshape(atoms, width),
        gain,
        up_weight,
        down_weight,
        *sums,
        keep=False,
    )
    return updated.reshape(features.shape)


def fits(mesh, features, wavevectors):
    count_x, count_y, count_z, tile, width = features
    per = mesh.shape["gx"] * mesh.shape["gz"]
    lengths = [n * GRID for n in (count_x, count_y, count_z)]
    return (
        count_x == mesh.shape["gx"]
        and count_y == mesh.shape["gy"]
        and tile == 128
        and width == 128
        and wavevectors[1] % (16 * per) == 0
        and all(n & (n - 1) == 0 and n <= 2**14 for n in lengths)
    )


def solution(mesh):
    in_specs = (
        P("gx", "gy", "gz", None, None),
        P(None, "gx", "gy", "gz", None),
        P(),
        P(),
        P(),
        P(),
        P(),
        P(),
        P(),
        P(),
    )
    out_specs = P("gx", "gy", "gz", None, None)

    def fast(*args):
        return fast_device(*args)

    def layer(*args):
        quick = fits(mesh, args[0].shape, args[2].shape)
        mapped = jax.shard_map(
            fast if quick else on_device,
            mesh=mesh,
            in_specs=in_specs,
            out_specs=out_specs,
            check_vma=False,
        )
        return mapped(*args)

    return layer
```
